32 devices in a mesh: region: 2 (over core), mx: 4 (over y, x), my: 4 (over z).
Axes of the slice: x: 2, y: 2, z: 4, core: 2. Of those that a mesh axis runs over, the one named last changes fastest.
Arguments:
- features_in: bfloat16 [2, 4, 4, 2, 16, 16, 16, 128], P('region', 'mx', 'my'), may hold values from -6 to 6
- conv_weight: bfloat16 [7, 128, 128], replicated, may hold values from -0.1875 to 0.1875
- conv_bias: float32 [128], replicated, may hold values from -3 to 3
- head_weight: bfloat16 [128, 128], replicated, may hold values from -0.5 to 0.5
- grad_out: bfloat16 [2, 4, 4, 2, 16, 16, 16, 128], P('region', 'mx', 'my'), may hold values from -6 to 6
- grad_head: bfloat16 [2, 4, 4, 256, 128], P('region', 'mx', 'my'), may hold values from -6 to 6
- block_count: int32 [2, 4, 4], P('region', 'mx', 'my'), may hold values from 1 to 2, as said below
- neighbours: int32 [2, 4, 4, 2, 6], P('region', 'mx', 'my'), may hold values from 0 to 2, as said below
Outputs:
- features_out: bfloat16 [2, 4, 4, 2, 16, 16, 16, 128], P('region', 'mx', 'my')
- head_out: bfloat16 [2, 4, 4, 256, 128], P('region', 'mx', 'my')
- grad_features: bfloat16 [2, 4, 4, 2, 16, 16, 16, 128], P('region', 'mx', 'my')
- grad_conv: float32 [7, 128, 128], replicated
- grad_bias: float32 [128], replicated
- grad_head_weight: float32 [128, 128], replicated
The draws below stay inside these ranges and needn't reach their ends.
Inputs may be any that keep to these rules, and one draw needn't show every extreme that they name: A tile's occupied blocks stand in slots 0 to block_count - 1; at least one tile holds exactly 2. `neighbours`: each occupied block has a height; slots of a tile hold rising heights. The -x and +x entries name the slot of the occupied block at the same height in the tile at mx index -1 and +1, the -y and +y entries likewise along my, the -z and +z entries the slot of the occupied block at height - 1 and + 1 in the same tile; 2 where there is no such block, beyond the map's edge and for every entry of an empty slot. Neighbours are mutual: the opposite face of a named block names the block back.
All inputs are finite; a program needn't handle non-finite values.
Results may differ from the reference program's by a relative error of at most 0.0085.
Values may be sent and summed in bfloat16 or wider, within the bound.
No kernel may reach another device: no remote copies, remote signals or barrier semaphores. Data moves between devices by JAX's collectives and lax.ppermute only.
A program may use at most 192 MiB of HBM per device.

```python
import jax
import jax.numpy as jnp
from jax import lax

C = 128
S = 16
NB = 2
REGIONS = 2
TILES_X = 4
TILES_Y = 4


def block_layout(key):
    layout_key = jax.random.fold_in(key, 41)
    key_count, key_full, key_levels = jax.random.split(layout_key, 3)
    levels = 2 * NB
    tile_shape = (REGIONS, TILES_X, TILES_Y)
    tile_total = REGIONS * TILES_X * TILES_Y
    counts = jax.random.randint(key_count, (tile_total,), 1, NB + 1)
    chosen = jax.random.randint(key_full, (), 0, tile_total)
    counts = jnp.where(jnp.arange(tile_total) == chosen, NB, counts).astype(jnp.int32).reshape(tile_shape)
    scores = jax.random.randint(key_levels, tile_shape + (levels,), 0, 1 << 20) * levels + jnp.arange(levels)
    ranking = jnp.argsort(scores, axis=-1, stable=True).astype(jnp.int32)
    slot_ids = jnp.arange(NB, dtype=jnp.int32)
    picked = jnp.where(slot_ids < counts[..., None], ranking[..., :NB], levels + slot_ids)
    heights = jnp.sort(picked, axis=-1).astype(jnp.int32)
    return (counts, heights)


def match_slots(others, targets, heights):
    equal_height = others[..., None, :] == targets[..., :, None]
    located = jnp.any(equal_height, axis=-1)
    slot_found = jnp.sum(jnp.where(equal_height, jnp.arange(NB, dtype=jnp.int32), 0), axis=-1).astype(jnp.int32)
    return jnp.where(located & (heights < 2 * NB), slot_found, NB).astype(jnp.int32)


def draw_block_count(key, part):
    counts, heights = block_layout(key)
    return counts


def draw_neighbours(key, part):
    counts, heights = block_layout(key)
    filler_x = jnp.full_like(heights[:, :1], 8 * NB)
    lower_x = jnp.concatenate([filler_x, heights[:, :-1]], axis=1)
    upper_x = jnp.concatenate([heights[:, 1:], filler_x], axis=1)
    filler_y = jnp.full_like(heights[:, :, :1], 8 * NB)
    lower_y = jnp.concatenate([filler_y, heights[:, :, :-1]], axis=2)
    upper_y = jnp.concatenate([heights[:, :, 1:], filler_y], axis=2)
    columns = [match_slots(lower_x, heights, heights), match_slots(upper_x, heights, heights), match_slots(lower_y, heights, heights), match_slots(upper_y, heights, heights), match_slots(heights, heights - 1, heights), match_slots(heights, heights + 1, heights)]
    return jnp.stack(columns, axis=-1).astype(jnp.int32)


def level_of(key, extent, cuts, low, top_value):
    factor_of, own = 1.0, jax.random.fold_in(key, 6)
    for position, shards_of in cuts:
        steps = jnp.exp(jax.random.uniform(jax.random.fold_in(own, position), (shards_of,), jnp.float32, low / len(cuts), top_value / len(cuts)))
        factor_of = factor_of * jnp.repeat(steps, extent[position] // shards_of).reshape([-1 if axis == position else 1 for axis in range(len(extent))])
    return factor_of


def normal_values(rng, extent, scale, most, pieces=(), kind=jnp.bfloat16):
    level = level_of(rng, extent, pieces, -0.22, 0.18) if pieces else 1.0
    drawn = jax.random.normal(rng, extent, jnp.float32) * scale * level
    return jnp.minimum(jnp.maximum(drawn, -most), most).astype(kind)


def setup_inputs(seed: int = 0) -> dict:
    key_list = jax.random.split(jax.random.key(seed), 9)
    features_in = normal_values(key_list[0], (REGIONS, TILES_X, TILES_Y, NB, S, S, S, C), 1.0, 6.0, ((0, 2), (1, 4), (2, 4)))
    conv_weight = normal_values(key_list[1], (7, C, C), (7 * C) ** -0.5, 0.1875)
    conv_bias = normal_values(key_list[2], (C,), 0.5, 3.0, (), jnp.float32)
    head_weight = normal_values(key_list[3], (C, C), C ** -0.5, 0.5)
    grad_out = normal_values(key_list[4], (REGIONS, TILES_X, TILES_Y, NB, S, S, S, C), 1.0, 6.0, ((0, 2), (1, 4), (2, 4)))
    grad_head = normal_values(key_list[5], (REGIONS, TILES_X, TILES_Y, S * S, C), 1.0, 6.0, ((0, 2), (1, 4), (2, 4)))
    block_count = draw_block_count(jax.random.fold_in(key_list[8], 71), 0)
    neighbours = draw_neighbours(jax.random.fold_in(key_list[8], 71), 0)
    return {"features_in": features_in, "conv_weight": conv_weight, "conv_bias": conv_bias, "head_weight": head_weight, "grad_out": grad_out, "grad_head": grad_head, "block_count": block_count, "neighbours": neighbours}


SHIFTS = ((0, 0, 0), (-1, 0, 0), (1, 0, 0), (0, -1, 0), (0, 1, 0), (0, 0, -1), (0, 0, 1))


def select_rows(layers, slot_index):
    zero_row = jnp.zeros((1,) + layers.shape[1:], layers.dtype)
    return jnp.take(jnp.concatenate([layers, zero_row], axis=0), slot_index, axis=0)


def pad_block(blocks, side_faces, links):
    padded = jnp.pad(blocks, ((0, 0), (1, 1), (1, 1), (1, 1), (0, 0)))
    padded = padded.at[:, 0, 1:-1, 1:-1].set(select_rows(side_faces[0], links[:, 0]))
    padded = padded.at[:, -1, 1:-1, 1:-1].set(select_rows(side_faces[1], links[:, 1]))
    padded = padded.at[:, 1:-1, 0, 1:-1].set(select_rows(side_faces[2], links[:, 2]))
    padded = padded.at[:, 1:-1, -1, 1:-1].set(select_rows(side_faces[3], links[:, 3]))
    padded = padded.at[:, 1:-1, 1:-1, 0].set(select_rows(blocks[:, :, :, -1], links[:, 4]))
    padded = padded.at[:, 1:-1, 1:-1, -1].set(select_rows(blocks[:, :, :, 0], links[:, 5]))
    return padded


def window(padded, shift):
    edge = padded.shape[1] - 2
    return padded[:, 1 + shift[0]:1 + shift[0] + edge, 1 + shift[1]:1 + shift[1] + edge, 1 + shift[2]:1 + shift[2] + edge]


def stencil(padded, conv_weight, direction):
    edge = padded.shape[1] - 2
    channels = padded.shape[-1]
    total = jnp.zeros((padded.shape[0] * edge * edge * edge, channels), jnp.float32)
    for offset_id in range(7):
        shift = tuple(direction * step for step in SHIFTS[offset_id])
        moved = window(padded, shift).reshape(-1, channels)
        matrix = conv_weight[offset_id] if direction > 0 else conv_weight[offset_id].T
        total = total + jnp.dot(moved, matrix, preferred_element_type=jnp.float32)
    return total.reshape(padded.shape[0], edge, edge, edge, channels)


def weight_terms(padded, grad_pre):
    channels = padded.shape[-1]
    rows = grad_pre.reshape(-1, channels)
    terms = []
    for offset_id in range(7):
        moved = window(padded, SHIFTS[offset_id]).reshape(-1, channels)
        terms.append(lax.dot_general(moved, rows, (((0,), (0,)), ((), ())), preferred_element_type=jnp.float32))
    return jnp.stack(terms, axis=0)


def side_layers(field):
    zeros_x = jnp.zeros_like(field[:, :1, :, :, 0])
    lower_x = jnp.concatenate([zeros_x, field[:, :-1, :, :, -1]], axis=1)
    upper_x = jnp.concatenate([field[:, 1:, :, :, 0], zeros_x], axis=1)
    zeros_y = jnp.zeros_like(field[:, :, :1, :, :, 0])
    lower_y = jnp.concatenate([zeros_y, field[:, :, :-1, :, :, -1]], axis=2)
    upper_y = jnp.concatenate([field[:, :, 1:, :, :, 0], zeros_y], axis=2)
    return (lower_x, upper_x, lower_y, upper_y)


def occupancy(total_blocks, slots):
    return (jnp.arange(slots) < total_blocks)[:, None, None, None, None]


def result_gradient(occupied, upstream_tile, column_tile, edge, channels):
    spread = column_tile.reshape(edge, edge, 1, channels)[None]
    return jnp.where(occupied, upstream_tile.astype(jnp.float32) + spread, 0.0)


def reference(features_in, conv_weight, conv_bias, head_weight, grad_out, grad_head, block_count, neighbours):
    grid_shape = features_in.shape
    device_total = grid_shape[0] * grid_shape[1] * grid_shape[2]
    edge = grid_shape[4]
    channels = grid_shape[-1]
    slots = grid_shape[3]

    def flatten(array):
        return array.reshape((device_total,) + array.shape[3:])

    input_sides = tuple(flatten(side) for side in side_layers(features_in))
    links_all = flatten(neighbours)
    totals_all = block_count.reshape(device_total)
    upstream_all = flatten(grad_out)
    head_grads = flatten(grad_head)
    blocks_all = flatten(features_in)

    def forward(items):
        blocks, side_one, side_two, side_three, side_four, links, total_blocks, upstream_tile, head_grad = items
        occupied = occupancy(total_blocks, slots)
        padded = pad_block(blocks, (side_one, side_two, side_three, side_four), links)
        preact = stencil(padded, conv_weight, 1) + conv_bias.astype(jnp.float32)
        result = jnp.where(occupied, blocks.astype(jnp.float32) + jax.nn.silu(preact), 0.0).astype(jnp.bfloat16)
        scale = 1.0 / (edge * total_blocks).astype(jnp.float32)
        column_mean = jnp.sum(result.astype(jnp.float32), axis=(0, 3)) * scale
        column_bf = column_mean.reshape(-1, channels).astype(jnp.bfloat16)
        head_tile = jnp.dot(column_bf, head_weight, preferred_element_type=jnp.float32).astype(jnp.bfloat16)
        column_grad = jnp.dot(head_grad, head_weight.T, preferred_element_type=jnp.float32) * scale
        grad_result = result_gradient(occupied, upstream_tile, column_grad, edge, channels)
        sigma = jax.nn.sigmoid(preact)
        grad_pre = jnp.where(occupied, grad_result * sigma * (1.0 + preact * (1.0 - sigma)), 0.0).astype(jnp.bfloat16)
        conv_part = weight_terms(padded, grad_pre)
        bias_part = jnp.sum(grad_pre.astype(jnp.float32), axis=(0, 1, 2, 3))
        head_part = lax.dot_general(column_bf, head_grad, (((0,), (0,)), ((), ())), preferred_element_type=jnp.float32)
        return result, head_tile, grad_pre, column_grad, conv_part, bias_part, head_part

    outputs = lax.map(forward, (blocks_all,) + input_sides + (links_all, totals_all, upstream_all, head_grads))
    features_out, head_out, grad_pre_all, column_grads, conv_parts, bias_parts, head_parts = outputs
    grad_sides = tuple(flatten(side) for side in side_layers(grad_pre_all.reshape(grid_shape)))

    def backward(items):
        grad_local, side_one, side_two, side_three, side_four, links, total_blocks, upstream_tile, column_grad = items
        occupied = occupancy(total_blocks, slots)
        grad_result = result_gradient(occupied, upstream_tile, column_grad, edge, channels)
        padded_grad = pad_block(grad_local, (side_one, side_two, side_three, side_four), links)
        return jnp.where(occupied, grad_result + stencil(padded_grad, conv_weight, -1), 0.0).astype(jnp.bfloat16)

    grad_features = lax.map(backward, (grad_pre_all,) + grad_sides + (links_all, totals_all, upstream_all, column_grads))
    return (features_out.reshape(grid_shape),
            head_out.reshape(grid_shape[:3] + head_out.shape[1:]),
            grad_features.reshape(grid_shape),
            jnp.sum(conv_parts, axis=0),
            jnp.sum(bias_parts, axis=0),
            jnp.sum(head_parts, axis=0))
```

```python
import functools

import jax
import jax.numpy as jnp
from jax import lax
from jax.experimental import pallas as pl
from jax.experimental.pallas import tpu as pltpu
from jax.sharding import PartitionSpec as P

BF = jnp.bfloat16
F32 = jnp.float32
PLANES = 4


def halo_copies(meta, parity, slots, faces, vol, sems):
    edge = vol.shape[1] - 2
    found = []
    for s in range(slots):
        for f in range(4):
            link = meta[4 + s * 6 + f]
            axis, upper = f // 2, f % 2
            at = edge + 1 if upper else 0
            if axis == 0:
                target = vol.at[s, at, 1 : edge + 1]
            else:
                target = vol.at[s, 1 : edge + 1, at]
            source = jnp.minimum(link, slots - 1)
            copies = [
                pltpu.make_async_copy(faces[2 * axis + ph].at[source], target, sems.at[s * 4 + f])
                for ph in range(2)
            ]
            phase = (parity[axis] + upper + 1) % 2
            found.append((link < slots, phase, copies, (s, f, at)))
    return found


def start_halos(found, vol):
    edge = vol.shape[1] - 2
    for valid, phase, copies, (s, f, at) in found:
        for ph in range(2):
            @pl.when(valid & (phase == ph))
            def _(copy=copies[ph]):
                copy.start()

        @pl.when(jnp.logical_not(valid))
        def _():
            if f < 2:
                vol[s, at, 1 : edge + 1] = jnp.zeros((edge, edge, vol.shape[4]), vol.dtype)
            else:
                vol[s, 1 : edge + 1, at] = jnp.zeros((edge, edge, vol.shape[4]), vol.dtype)


def wait_halos(found):
    for valid, _, copies, _ in found:
        @pl.when(valid)
        def _(copy=copies[0]):
            copy.wait()


def windows(meta, vol, zbuf, s, x0, slots, direction):
    edge = vol.shape[1] - 2
    channels = vol.shape[4]
    rows = PLANES * edge * edge

    def at(dx, dy):
        return vol[s, pl.ds(x0 + 1 + dx, PLANES), 1 + dy : 1 + dy + edge]

    centre = at(0, 0)

    def beyond(face, part):
        link = meta[4 + s * 6 + face]
        other = vol[jnp.minimum(link, slots - 1), pl.ds(x0 + 1, PLANES), 1 : 1 + edge]
        other = other.astype(F32).reshape(PLANES * edge, edge, channels)[:, part]
        return jnp.where(link < slots, other, 0.0)

    zbuf[:, 0:8] = beyond(4, slice(edge - 8, edge))
    zbuf[:, 8 : 8 + edge] = centre.astype(F32).reshape(PLANES * edge, edge, channels)
    zbuf[:, 8 + edge : 16 + edge] = beyond(5, slice(0, 8))
    below = zbuf[:, 7 : 7 + edge].astype(BF)
    above = zbuf[:, 9 : 9 + edge].astype(BF)
    d = direction
    pieces = [centre, at(-d, 0), at(d, 0), at(0, -d), at(0, d)]
    pieces += [below, above] if d > 0 else [above, below]
    return jnp.concatenate([piece.reshape(rows, channels) for piece in pieces], axis=1)


def forward_kernel(
    meta, feat, x0f, x1f, y0f, y1f, w, bias, hw, gout, ghead,
    res_o, head_o, gpre_o, gx_o, gy_o, colg_o, pay_o,
    vol, zbuf, colsum, sems,
):
    slots, edge, channels = feat.shape[0], feat.shape[1], feat.shape[4]
    s, xi = pl.program_id(0), pl.program_id(1)
    steps = edge // PLANES
    count = meta[0]
    scale = 1.0 / (edge * count).astype(F32)
    taps = w.shape[0] // channels

    @pl.when((s == 0) & (xi == 0))
    def _():
        body = [
            pltpu.make_async_copy(
                feat.at[i], vol.at[i, 1 : edge + 1, 1 : edge + 1], sems.at[slots * 4 + i]
            )
            for i in range(slots)
        ]
        found = halo_copies(meta, (meta[1], meta[2]), slots, (x0f, x1f, y0f, y1f), vol, sems)
        for copy in body:
            copy.start()
        start_halos(found, vol)
        colg_o[...] = (
            lax.dot_general(
                ghead[...], hw[...], (((1,), (1,)), ((), ())), preferred_element_type=F32
            )
            * scale
        )
        pay_o[...] = jnp.zeros_like(pay_o)
        colsum[...] = jnp.zeros_like(colsum)
        for copy in body:
            copy.wait()
        wait_halos(found)

    x0 = xi * PLANES
    rows = PLANES * edge * edge
    cols = PLANES * edge
    stacked = windows(meta, vol, zbuf, s, x0, slots, 1)
    preact = jnp.dot(stacked, w[...], preferred_element_type=F32) + bias[...]
    occupied = s < count
    sigma = 0.5 * jnp.tanh(0.5 * preact) + 0.5
    silu = preact * sigma
    result = jnp.where(occupied, stacked[:, :channels].astype(F32) + silu, 0.0).astype(BF)
    res_o[0] = result.reshape(PLANES, edge, edge, channels)
    column = pl.ds(pl.multiple_of(x0 * edge, cols), cols)
    spread = colg_o[column].reshape(cols, 1, channels)
    grad_result = gout[0].astype(F32).reshape(cols, edge, channels) + spread
    slope = sigma * (1.0 + (preact - silu))
    gpre = jnp.where(occupied, grad_result.reshape(rows, channels) * slope, 0.0).astype(BF)
    gtile = gpre.reshape(PLANES, edge, edge, channels)
    gpre_o[0] = gtile

    @pl.when(xi == 0)
    def _():
        gx_o[0, s] = gtile[0]

    @pl.when(xi == steps - 1)
    def _():
        gx_o[1, s] = gtile[PLANES - 1]

    gy_o[0, s, pl.ds(x0, PLANES)] = gtile[:, 0]
    gy_o[1, s, pl.ds(x0, PLANES)] = gtile[:, edge - 1]

    of_row = lax.broadcasted_iota(jnp.int32, (cols, rows), 1) // edge
    pool = (of_row == lax.broadcasted_iota(jnp.int32, (cols, rows), 0)).astype(BF)
    colsum[column] += jnp.dot(pool, result, preferred_element_type=F32)
    pay_o[0 : taps * channels] += lax.dot_general(
        stacked, gpre, (((0,), (0,)), ((), ())), preferred_element_type=F32
    )
    ones = jnp.ones((16, rows), BF)
    tail = (taps + 1) * channels
    pay_o[tail : tail + 16] += jnp.dot(ones, gpre, preferred_element_type=F32)

    @pl.when((s == slots - 1) & (xi == steps - 1))
    def _():
        column_bf = (colsum[...] * scale).astype(BF)
        head_o[...] = jnp.dot(column_bf, hw[...], preferred_element_type=F32).astype(BF)
        pay_o[taps * channels : tail] = lax.dot_general(
            column_bf, ghead[...], (((0,), (0,)), ((), ())), preferred_element_type=F32
        )


def backward_kernel(meta, grad, x0f, x1f, y0f, y1f, wt, gout, colg, out_o, vol, zbuf, sems):
    slots, edge, channels = grad.shape[0], grad.shape[1], grad.shape[4]
    s, xi = pl.program_id(0), pl.program_id(1)

    @pl.when((s == 0) & (xi == 0))
    def _():
        body = [
            pltpu.make_async_copy(
                grad.at[i], vol.at[i, 1 : edge + 1, 1 : edge + 1], sems.at[slots * 4 + i]
            )
            for i in range(slots)
        ]
        found = halo_copies(meta, (meta[1], meta[2]), slots, (x0f, x1f, y0f, y1f), vol, sems)
        for copy in body:
            copy.start()
        start_halos(found, vol)
        for copy in body:
            copy.wait()
        wait_halos(found)

    x0 = xi * PLANES
    rows = PLANES * edge * edge
    cols = PLANES * edge
    stacked = windows(meta, vol, zbuf, s, x0, slots, -1)
    conv = jnp.dot(stacked, wt[...], preferred_element_type=F32)
    column = pl.ds(pl.multiple_of(x0 * edge, cols), cols)
    spread = colg[column].reshape(cols, 1, channels)
    grad_result = gout[0].astype(F32).reshape(cols, edge, channels) + spread
    total = jnp.where(s < meta[0], grad_result.reshape(rows, channels) + conv, 0.0).astype(BF)
    out_o[0] = total.reshape(PLANES, edge, edge, channels)


def swap(x, axis, odd):
    pairs = []
    for i in range(odd, lax.axis_size(axis) - 1, 2):
        pairs += [(i, i + 1), (i + 1, i)]
    return lax.ppermute(x, axis, pairs)


def swap_faces(low_high, axis):
    parity = lax.axis_index(axis) % 2
    arrived = []
    for odd in range(2):
        upward = parity == odd
        arrived.append(swap(jnp.where(upward, low_high[1], low_high[0]), axis, odd))
    return arrived


def partner(x, axis, bit):
    return lax.ppermute(x, axis, [(i, i ^ (1 << bit)) for i in range(lax.axis_size(axis))])


def own_bit(axis, bit):
    return (lax.axis_index(axis) >> bit) & 1


def halved(x, axis, bit):
    me = own_bit(axis, bit)
    parts = x.reshape((2, x.shape[0] // 2) + x.shape[1:])
    own = lax.dynamic_index_in_dim(parts, me, 0, False)
    sent = lax.dynamic_index_in_dim(parts, 1 - me, 0, False)
    return own + partner(sent.astype(BF), axis, bit).astype(F32)


def summed(x, axis, bit):
    return x + partner(x.astype(BF), axis, bit).astype(F32)


def doubled(x, axis, bit):
    other = partner(x, axis, bit)
    return jnp.where(
        own_bit(axis, bit) == 0, jnp.concatenate([x, other]), jnp.concatenate([other, x])
    )


def bits(axis):
    return range((lax.axis_size(axis) - 1).bit_length())


def all_summed(x):
    split = [("region", b) for b in bits("region")] + [("my", 0)]
    rest = [("my", b) for b in bits("my")][1:] + [("mx", b) for b in bits("mx")]
    for axis, bit in split:
        x = halved(x, axis, bit)
    for axis, bit in rest:
        x = summed(x, axis, bit)
    x = x.astype(BF)
    for axis, bit in reversed(split):
        x = doubled(x, axis, bit)
    return x.astype(F32)


def body(
    features_in, conv_weight, conv_bias, head_weight, grad_out, grad_head, block_count, neighbours
):
    blocks = features_in.reshape(features_in.shape[3:])
    upstream = grad_out.reshape(grad_out.shape[3:])
    head_grad = grad_head.reshape(grad_head.shape[3:])
    slots, edge, channels = blocks.shape[0], blocks.shape[1], blocks.shape[4]
    taps = conv_weight.shape[0]
    steps = edge // PLANES
    meta = jnp.concatenate(
        [
            block_count.reshape(1),
            (lax.axis_index("mx") % 2).astype(jnp.int32).reshape(1),
            (lax.axis_index("my") % 2).astype(jnp.int32).reshape(1),
            jnp.zeros((1,), jnp.int32),
            neighbours.reshape(-1),
        ]
    )
    faces = swap_faces((blocks[:, 0], blocks[:, -1]), "mx")
    faces += swap_faces((blocks[:, :, 0], blocks[:, :, -1]), "my")

    whole = lambda *shape: pl.BlockSpec(shape, lambda i, j, m: (0,) * len(shape))
    tile = pl.BlockSpec(
        (1, PLANES, edge, edge, channels), lambda i, j, m: (i, j, 0, 0, 0)
    )
    anywhere = pl.BlockSpec(memory_space=pl.ANY)
    volume = (slots, edge, edge, edge, channels)
    padded = pltpu.VMEM((slots, edge + 2, edge + 2, edge, channels), BF)
    zscratch = pltpu.VMEM((PLANES * edge, edge + 16, channels), F32)
    columns = edge * edge
    pay_rows = ((taps + 1) * channels // 64 + 1) * 64
    flops = 2 * slots * edge**3 * taps * channels * channels
    moved = slots * edge**3 * channels * 2
    params = pltpu.CompilerParams(
        dimension_semantics=("arbitrary", "arbitrary"), vmem_limit_bytes=48 << 20
    )
    result, head_tile, gpre, gx, gy, colg, pay = pl.pallas_call(
        forward_kernel,
        grid_spec=pltpu.PrefetchScalarGridSpec(
            num_scalar_prefetch=1,
            grid=(slots, steps),
            in_specs=[
                anywhere, anywhere, anywhere, anywhere, anywhere,
                whole(taps * channels, channels), whole(1, channels), whole(channels, channels),
                tile, whole(columns, channels),
            ],
            out_specs=[
                tile, whole(columns, channels), tile,
                whole(2, slots, edge, edge, channels), whole(2, slots, edge, edge, channels),
                whole(columns, channels), whole(pay_rows, channels),
            ],
            scratch_shapes=[
                padded, zscratch, pltpu.VMEM((columns, channels), F32),
                pltpu.SemaphoreType.DMA((slots * 5,)),
            ],
        ),
        out_shape=[
            jax.ShapeDtypeStruct(volume, BF),
            jax.ShapeDtypeStruct((columns, channels), BF),
            jax.ShapeDtypeStruct(volume, BF),
            jax.ShapeDtypeStruct((2, slots, edge, edge, channels), BF),
            jax.ShapeDtypeStruct((2, slots, edge, edge, channels), BF),
            jax.ShapeDtypeStruct((columns, channels), F32),
            jax.ShapeDtypeStruct((pay_rows, channels), F32),
        ],
        compiler_params=params,
        cost_estimate=pl.CostEstimate(
            flops=2 * flops, bytes_accessed=5 * moved, transcendentals=moved // 2
        ),
        name="forward",
    )(
        meta, blocks, *faces, conv_weight.reshape(taps * channels, channels),
        conv_bias.reshape(1, channels), head_weight, upstream, head_grad,
    )

    grad_faces = swap_faces(gx, "mx") + swap_faces(gy, "my")
    turned = jnp.transpose(conv_weight, (0, 2, 1)).reshape(taps * channels, channels)
    grad_local = pl.pallas_call(
        backward_kernel,
        grid_spec=pltpu.PrefetchScalarGridSpec(
            num_scalar_prefetch=1,
            grid=(slots, steps),
            in_specs=[
                anywhere, anywhere, anywhere, anywhere, anywhere,
                whole(taps * channels, channels), tile, whole(columns, channels),
            ],
            out_specs=tile,
            scratch_shapes=[padded, zscratch, pltpu.SemaphoreType.DMA((slots * 5,))],
        ),
        out_shape=jax.ShapeDtypeStruct(volume, BF),
        compiler_params=params,
        cost_estimate=pl.CostEstimate(
            flops=flops, bytes_accessed=4 * moved, transcendentals=0
        ),
        name="backward",
    )(meta, gpre, *grad_faces, turned, upstream, colg)

    total = all_summed(pay)
    conv_rows = taps * channels
    return (
        result.reshape(features_in.shape),
        head_tile.reshape(grad_head.shape),
        grad_local.reshape(features_in.shape),
        total[:conv_rows].reshape(taps, channels, channels),
        total[conv_rows + channels],
        total[conv_rows : conv_rows + channels],
    )


def solution(mesh):
    tiles = P("region", "mx", "my", None, None, None, None, None)
    rows = P("region", "mx", "my", None, None)
    return jax.shard_map(
        body,
        mesh=mesh,
        in_specs=(tiles, P(), P(), P(), tiles, rows, P("region", "mx", "my"), rows),
        out_specs=(tiles, rows, tiles, P(), P(), P()),
        check_vma=False,
    )
```

```python
import functools

import jax
import jax.numpy as jnp
from jax import lax
from jax.experimental import pallas as pl
from jax.experimental.pallas import tpu as pltpu
from jax.sharding import PartitionSpec as P


BF = jnp.bfloat16
F32 = jnp.float32
PLANES = 8
PIECE = 16
GRANT = 60 * 1024 * 1024


def halo_copies(meta, slots, faces, vol, sems, first, planes, edge):
    found = []
    for s in range(slots):
        for f in range(4):
            link = meta[4 + s * 6 + f]
            axis, upper = f // 2, f % 2
            if axis == 0 and first + (planes if upper else 0) != (edge if upper else 0):
                continue
            source = jnp.minimum(link, slots - 1)
            if axis == 0:
                index = (s, planes + 1 if upper else 0, slice(1, edge + 1))
                arrived = [faces[ph].at[source] for ph in range(2)]
            else:
                index = (s, slice(1, planes + 1), edge + 1 if upper else 0)
                arrived = [faces[2 + ph].at[source, first : first + planes] for ph in range(2)]
            copies = [
                pltpu.make_async_copy(arrived[ph], vol.at[index], sems.at[s * 4 + f])
                for ph in range(2)
            ]
            phase = (meta[1 + axis] + upper + 1) % 2
            found.append((link < slots, phase, copies, index))
    return found


def start_halos(found, vol):
    for valid, phase, copies, index in found:
        for ph in range(2):
            @pl.when(valid & (phase == ph))
            def _(copy=copies[ph]):
                copy.start()

        @pl.when(jnp.logical_not(valid))
        def _(index=index):
            vol[index] = jnp.zeros(vol.at[index].shape, vol.dtype)


def wait_halos(found):
    for valid, _, copies, _ in found:
        @pl.when(valid)
        def _(copy=copies[0]):
            copy.wait()


def shifted(vol, s, x0, planes, dx, dy):
    edge = vol.shape[2] - 2
    view = vol[s, pl.ds(x0 + 1 + dx, planes), 1 + dy : 1 + dy + edge]
    return view.reshape(planes * edge * edge, vol.shape[4])


def z_shifted(meta, vol, zbuf, s, x0, planes):
    slots, edge, channels = vol.shape[0], vol.shape[2] - 2, vol.shape[4]
    rows = planes * edge * edge

    def beyond(face, part):
        link = meta[4 + s * 6 + face]
        other = vol[jnp.minimum(link, slots - 1), pl.ds(x0 + 1, planes), 1 : 1 + edge]
        other = other.astype(F32).reshape(planes * edge, edge, channels)[:, part]
        return jnp.where(link < slots, other, 0.0)

    centre = shifted(vol, s, x0, planes, 0, 0)
    zbuf[:, 0:8] = beyond(4, slice(edge - 8, edge))
    zbuf[:, 8 : 8 + edge] = centre.astype(F32).reshape(planes * edge, edge, channels)
    zbuf[:, 8 + edge : 16 + edge] = beyond(5, slice(0, 8))
    below = zbuf[:, 7 : 7 + edge].astype(BF).reshape(rows, channels)
    above = zbuf[:, 9 : 9 + edge].astype(BF).reshape(rows, channels)
    return below, above


def windows(meta, vol, zbuf, s, x0, planes, direction):
    below, above = z_shifted(meta, vol, zbuf, s, x0, planes)
    d = direction
    pieces = [
        shifted(vol, s, x0, planes, dx, dy)
        for dx, dy in ((0, 0), (-d, 0), (d, 0), (0, -d), (0, d))
    ]
    pieces += [below, above] if d > 0 else [above, below]
    return jnp.concatenate(pieces, axis=1)


def add_weight_terms(acc, turned, vol, zlow, zhigh, s, x0, planes):
    channels = vol.shape[4]
    near = [(0, 0), (-1, 0), (1, 0), (0, -1), (0, 1)]
    pieces = [lambda d=d: shifted(vol, s, x0, planes, *d) for d in near]
    pieces += [lambda: zlow[...], lambda: zhigh[...]]
    left = turned[...]
    for t in range(0, len(pieces), 2):
        right = jnp.concatenate([piece() for piece in pieces[t : t + 2]], axis=1)
        at = slice(t * channels, t * channels + right.shape[1])
        acc[:, at] += jnp.dot(left, right, preferred_element_type=F32)


def pick_kernel(feat, x0, x1, y0, y1, sems):
    edge = feat.shape[1]
    copies = []
    for i, out in enumerate((x0, x1, y0, y1)):
        upward = lax.axis_index(("mx", "my")[i // 2]) % 2 == i % 2
        layer = jnp.where(upward, edge - 1, 0)
        face = feat.at[:, layer] if i < 2 else feat.at[:, :, layer]
        copies.append(pltpu.make_async_copy(face, out, sems.at[i]))
    for copy in copies:
        copy.start()
    for copy in copies:
        copy.wait()


def finish_kernel(meta, own, other, conv_o, bias_o, head_o):
    half = own.shape[0]
    edges = (conv_o.shape[0], conv_o.shape[0] + head_o.shape[0])

    def place(h, value):
        lo = h * half
        n = min(max(edges[0] - lo, 0), half)
        if n:
            conv_o[lo : lo + n] = value[:n]
        start, stop = max(edges[0] - lo, 0), min(edges[1] - lo, half)
        if start < stop:
            at = lo + start - edges[0]
            head_o[at : at + stop - start] = value[start:stop]
        if 0 <= edges[1] - lo < half:
            bias_o[...] = value[edges[1] - lo : edges[1] - lo + 1]

    first = meta[3] == 0
    place(0, jnp.where(first, own[...], other[...]).astype(F32))
    place(1, jnp.where(first, other[...], own[...]).astype(F32))


def forward_kernel(
    meta, feat, x0f, x1f, y0f, y1f, w, bias, hw, gout, ghead,
    res_o, head_o, gpre_o, gx0_o, gx1_o, gy0_o, gy1_o, colg_o, pay_o,
    vol, zbuf, colsum, acc, turned, zlow, zhigh, sems,
):
    slots, edge, channels = feat.shape[0], feat.shape[1], feat.shape[4]
    s, xi = pl.program_id(0), pl.program_id(1)
    planes = res_o.shape[1]
    steps = edge // planes
    count = meta[0]
    scale = 1.0 / (edge * count).astype(F32)
    taps = w.shape[0] // channels

    @pl.when((s == 0) & (xi == 0))
    def _():
        body = [
            pltpu.make_async_copy(
                feat.at[i], vol.at[i, 1 : edge + 1, 1 : edge + 1], sems.at[slots * 4 + i]
            )
            for i in range(slots)
        ]
        found = halo_copies(meta, slots, (x0f, x1f, y0f, y1f), vol, sems, 0, edge, edge)
        for copy in body:
            copy.start()
        start_halos(found, vol)
        colg_o[...] = (
            lax.dot_general(
                ghead[...], hw[...], (((1,), (1,)), ((), ())), preferred_element_type=F32
            )
            * scale
        )
        pay_o[...] = jnp.zeros_like(pay_o)
        for ref in (acc, turned, zlow, zhigh):
            ref[...] = jnp.zeros_like(ref)
        colsum[...] = jnp.zeros_like(colsum)
        for copy in body:
            copy.wait()
        wait_halos(found)

    x0 = xi * planes
    rows = planes * edge * edge
    cols = planes * edge
    before_s = jnp.maximum(jnp.where(xi == 0, s - 1, s), 0)
    before_x0 = jnp.where(xi == 0, edge - planes, x0 - planes)
    add_weight_terms(acc, turned, vol, zlow, zhigh, before_s, before_x0, planes)
    stacked = windows(meta, vol, zbuf, s, x0, planes, 1)
    preact = jnp.dot(stacked, w[...], preferred_element_type=F32) + bias[...]
    occupied = s < count
    sigma = 0.5 * jnp.tanh(0.5 * preact) + 0.5
    silu = preact * sigma
    result = jnp.where(occupied, stacked[:, :channels].astype(F32) + silu, 0.0).astype(BF)
    res_o[0] = result.reshape(planes, edge, edge, channels)
    column = pl.ds(pl.multiple_of(x0 * edge, cols), cols)
    spread = colg_o[column].reshape(cols, 1, channels)
    grad_result = gout[0].astype(F32).reshape(cols, edge, channels) + spread
    slope = sigma * (1.0 + (preact - silu))
    gpre = jnp.where(occupied, grad_result.reshape(rows, channels) * slope, 0.0).astype(BF)
    gtile = gpre.reshape(planes, edge, edge, channels)
    gpre_o[0] = gtile
    for upper, step, layer in ((0, 0, 0), (1, steps - 1, planes - 1)):
        for phase, out in ((0, gx0_o), (1, gx1_o)):
            @pl.when((xi == step) & ((meta[1] == phase) == bool(upper)))
            def _(out=out, layer=layer):
                out[s] = gtile[layer]

    even = meta[2] == 0
    low, high = gtile[:, 0], gtile[:, edge - 1]
    gy0_o[s, pl.ds(x0, planes)] = jnp.where(even, high, low)
    gy1_o[s, pl.ds(x0, planes)] = jnp.where(even, low, high)

    of_row = lax.broadcasted_iota(jnp.int32, (cols, rows), 1) // edge
    pool = (of_row == lax.broadcasted_iota(jnp.int32, (cols, rows), 0)).astype(BF)
    colsum[column] += jnp.dot(pool, result, preferred_element_type=F32)
    tail = (taps + 1) * channels
    pay_o[tail : tail + 1] += jnp.sum(gpre.astype(F32), axis=0, keepdims=True)
    turned[...] = gpre.T
    zlow[...] = stacked[:, 5 * channels : 6 * channels]
    zhigh[...] = stacked[:, 6 * channels : 7 * channels]

    @pl.when((s == slots - 1) & (xi == steps - 1))
    def _():
        add_weight_terms(acc, turned, vol, zlow, zhigh, s, x0, planes)
        for t in range(taps):
            at = slice(t * channels, (t + 1) * channels)
            pay_o[at] = acc[:, at].T
        column_bf = (colsum[...] * scale).astype(BF)
        head_o[...] = jnp.dot(column_bf, hw[...], preferred_element_type=F32).astype(BF)
        pay_o[taps * channels : tail] = lax.dot_general(
            column_bf, ghead[...], (((0,), (0,)), ((), ())), preferred_element_type=F32
        )


def backward_kernel(first, meta, grad, x0f, x1f, y0f, y1f, wt, gout, colg, *rest):
    out_o, vol, zbuf, sems = rest[-4:]
    slots, edge, channels = grad.shape[0], grad.shape[1], grad.shape[4]
    planes = gout.shape[1]
    s = pl.program_id(0)

    @pl.when(s == 0)
    def _():
        below, above = min(first, 1), min(edge - first - planes, 1)
        body = [
            pltpu.make_async_copy(
                grad.at[i, first - below : first + planes + above],
                vol.at[i, 1 - below : 1 + planes + above, 1 : edge + 1],
                sems.at[slots * 4 + i],
            )
            for i in range(slots)
        ]
        found = halo_copies(meta, slots, (x0f, x1f, y0f, y1f), vol, sems, first, planes, edge)
        for copy in body:
            copy.start()
        start_halos(found, vol)
        for copy in body:
            copy.wait()
        wait_halos(found)

    rows = planes * edge * edge
    cols = planes * edge
    stacked = windows(meta, vol, zbuf, s, 0, planes, -1)
    conv = jnp.dot(stacked, wt[...], preferred_element_type=F32)
    spread = colg[first * edge : first * edge + cols].reshape(cols, 1, channels)
    grad_result = gout[0].astype(F32).reshape(cols, edge, channels) + spread
    total = jnp.where(s < meta[0], grad_result.reshape(rows, channels) + conv, 0.0).astype(BF)
    out_o[0] = total.reshape(planes, edge, edge, channels)


def swap(x, axis, odd):
    pairs = []
    for i in range(odd, lax.axis_size(axis) - 1, 2):
        pairs += [(i, i + 1), (i + 1, i)]
    return lax.ppermute(x, axis, pairs)


def swap_faces(sent, axis):
    arrived = []
    for odd in range(2):
        arrived.append(swap(sent[odd], axis, odd))
    return arrived


def partner(x, axis, bit):
    return lax.ppermute(x, axis, [(i, i ^ (1 << bit)) for i in range(lax.axis_size(axis))])


def own_bit(axis, bit):
    return (lax.axis_index(axis) >> bit) & 1


def halved(x, axis, bit):
    me = own_bit(axis, bit)
    parts = x.reshape((2, x.shape[0] // 2) + x.shape[1:])
    own = lax.dynamic_index_in_dim(parts, me, 0, False)
    sent = lax.dynamic_index_in_dim(parts, 1 - me, 0, False)
    return own + partner(sent.astype(BF), axis, bit).astype(F32)


def summed(x, axis, bit):
    return x + partner(x.astype(BF), axis, bit).astype(F32)


def doubled(x, axis, bit):
    other = partner(x, axis, bit)
    return jnp.where(
        own_bit(axis, bit) == 0, jnp.concatenate([x, other]), jnp.concatenate([other, x])
    )


def bits(axis):
    return range((lax.axis_size(axis) - 1).bit_length())


def all_summed(x):
    x = halved(x, "region", 0)
    x = halved(x, "my", 0)
    rest = [(axis, b) for axis in ("mx", "my") for b in bits(axis)]
    rest.remove(("my", 0))
    for axis, bit in sorted(rest, key=lambda stage: stage[1]):
        x = summed(x, axis, bit)
    x = doubled(x.astype(BF), "my", 0)
    return x, partner(x, "region", 0)


def body(
    features_in, conv_weight, conv_bias, head_weight, grad_out, grad_head, block_count, neighbours
):
    blocks = features_in.reshape(features_in.shape[3:])
    upstream = grad_out.reshape(grad_out.shape[3:])
    head_grad = grad_head.reshape(grad_head.shape[3:])
    slots, edge, channels = blocks.shape[0], blocks.shape[1], blocks.shape[4]
    taps = conv_weight.shape[0]
    meta = jnp.concatenate(
        [
            block_count.reshape(1),
            (lax.axis_index("mx") % 2).astype(jnp.int32).reshape(1),
            (lax.axis_index("my") % 2).astype(jnp.int32).reshape(1),
            lax.axis_index("region").astype(jnp.int32).reshape(1),
            neighbours.reshape(-1),
        ]
    )
    anywhere = pl.BlockSpec(memory_space=pl.ANY)
    hbm = pl.BlockSpec(memory_space=pltpu.HBM)
    vmem = pl.BlockSpec(memory_space=pltpu.VMEM)
    face = jax.ShapeDtypeStruct((slots, edge, edge, channels), BF)
    sent = pl.pallas_call(
        pick_kernel,
        in_specs=[hbm],
        out_specs=[vmem] * 4,
        scratch_shapes=[pltpu.SemaphoreType.DMA((4,))],
        out_shape=[face] * 4,
        name="pick",
    )(blocks)
    faces = swap_faces(sent[:2], "mx") + swap_faces(sent[2:], "my")

    whole = lambda *shape: pl.BlockSpec(shape, lambda i, j, m: (0,) * len(shape))
    tile = pl.BlockSpec((1, PLANES, edge, edge, channels), lambda i, j, m: (i, j, 0, 0, 0))
    volume = (slots, edge, edge, edge, channels)
    padded = pltpu.VMEM((slots, edge + 2, edge + 2, edge, channels), BF)
    columns = edge * edge
    pay_rows = ((taps + 1) * channels // 64 + 1) * 64
    flops = 2 * slots * edge**3 * taps * channels * channels
    moved = slots * edge**3 * channels * 2
    params = pltpu.CompilerParams(
        dimension_semantics=("arbitrary", "arbitrary"), vmem_limit_bytes=GRANT
    )
    result, head_tile, gpre, gx0, gx1, gy0, gy1, colg, pay = pl.pallas_call(
        forward_kernel,
        grid_spec=pltpu.PrefetchScalarGridSpec(
            num_scalar_prefetch=1,
            grid=(slots, edge // PLANES),
            in_specs=[
                hbm, anywhere, anywhere, anywhere, anywhere,
                whole(taps * channels, channels), whole(1, channels), whole(channels, channels),
                tile, whole(columns, channels),
            ],
            out_specs=[
                tile, whole(columns, channels), tile,
                *[whole(slots, edge, edge, channels)] * 4,
                whole(columns, channels), whole(pay_rows, channels),
            ],
            scratch_shapes=[
                padded, pltpu.VMEM((PLANES * edge, edge + 16, channels), F32),
                pltpu.VMEM((columns, channels), F32),
                pltpu.VMEM((channels, taps * channels), F32),
                pltpu.VMEM((channels, PLANES * columns), BF),
                pltpu.VMEM((PLANES * columns, channels), BF),
                pltpu.VMEM((PLANES * columns, channels), BF),
                pltpu.SemaphoreType.DMA((slots * 5,)),
            ],
        ),
        out_shape=[
            jax.ShapeDtypeStruct(volume, BF),
            jax.ShapeDtypeStruct((columns, channels), BF),
            jax.ShapeDtypeStruct(volume, BF),
            *[face] * 4,
            jax.ShapeDtypeStruct((columns, channels), F32),
            jax.ShapeDtypeStruct((pay_rows, channels), F32),
        ],
        compiler_params=params,
        cost_estimate=pl.CostEstimate(
            flops=2 * flops, bytes_accessed=5 * moved, transcendentals=moved // 2
        ),
        name="forward",
    )(
        meta, blocks, *faces, conv_weight.reshape(taps * channels, channels),
        conv_bias.reshape(1, channels), head_weight, upstream, head_grad,
    )

    grad_faces = swap_faces((gx0, gx1), "mx") + swap_faces((gy0, gy1), "my")
    turned = jnp.transpose(conv_weight, (0, 2, 1)).reshape(taps * channels, channels)
    grad_local = None
    pieces = edge // PIECE
    for k in range(pieces):
        part = pl.BlockSpec((1, PIECE, edge, edge, channels), lambda i, m, k=k: (i, k, 0, 0, 0))
        all_of = lambda *shape: pl.BlockSpec(shape, lambda i, m: (0,) * len(shape))
        operands = [meta, gpre, *grad_faces, turned, upstream, colg]
        specs = [hbm] + [anywhere] * 4
        specs += [all_of(taps * channels, channels), part, all_of(columns, channels)]
        if grad_local is not None:
            operands.append(grad_local)
            specs.append(hbm)
        grad_local = pl.pallas_call(
            functools.partial(backward_kernel, k * PIECE),
            grid_spec=pltpu.PrefetchScalarGridSpec(
                num_scalar_prefetch=1,
                grid=(slots,),
                in_specs=specs,
                out_specs=part,
                scratch_shapes=[
                    pltpu.VMEM((slots, PIECE + 2, edge + 2, edge, channels), BF),
                    pltpu.VMEM((PIECE * edge, edge + 16, channels), F32),
                    pltpu.SemaphoreType.DMA((slots * 5,)),
                ],
            ),
            out_shape=jax.ShapeDtypeStruct(volume, BF),
            input_output_aliases={len(operands) - 1: 0} if k else {},
            compiler_params=pltpu.CompilerParams(
                dimension_semantics=("arbitrary",), vmem_limit_bytes=GRANT
            ),
            cost_estimate=pl.CostEstimate(
                flops=flops // pieces, bytes_accessed=4 * moved // pieces, transcendentals=0
            ),
        )(*operands)

    own, other = all_summed(pay)
    conv_rows = taps * channels
    grad_conv, grad_bias, grad_head_weight = pl.pallas_call(
        finish_kernel,
        grid_spec=pltpu.PrefetchScalarGridSpec(
            num_scalar_prefetch=1, grid=(), in_specs=[vmem] * 2, out_specs=[vmem] * 3
        ),
        out_shape=[
            jax.ShapeDtypeStruct((conv_rows, channels), F32),
            jax.ShapeDtypeStruct((1, channels), F32),
            jax.ShapeDtypeStruct((channels, channels), F32),
        ],
        name="finish",
    )(meta, own, other)
    return (
        result.reshape(features_in.shape),
        head_tile.reshape(grad_head.shape),
        grad_local.reshape(features_in.shape),
        grad_conv.reshape(conv_weight.shape),
        grad_bias.reshape(channels),
        grad_head_weight,
    )


def solution(mesh):
    tiles = P("region", "mx", "my", None, None, None, None, None)
    rows = P("region", "mx", "my", None, None)

    return jax.shard_map(
        body,
        mesh=mesh,
        in_specs=(tiles, P(), P(), P(), tiles, rows, P("region", "mx", "my"), rows),
        out_specs=(tiles, rows, tiles, P(), P(), P()),
        check_vma=False,
    )
```

```python
import functools

import jax
import jax.numpy as jnp
from jax import lax
from jax.experimental import pallas as pl
from jax.experimental.pallas import tpu as pltpu
from jax.sharding import PartitionSpec as P


BF = jnp.bfloat16
F32 = jnp.float32
PLANES = 8
PIECE = 16
STEP = 8
GRANT = 44 << 20


def halo_copies(meta, slots, faces, vol, sems, first, planes, edge):
    found = []
    for s in range(slots):
        for f in range(4):
            link = meta[s * 6 + f]
            axis, upper = f // 2, f % 2
            if axis == 0 and first + (planes if upper else 0) != (edge if upper else 0):
                continue
            source = jnp.minimum(link, slots - 1)
            if axis == 0:
                index = (s, planes + 1 if upper else 0, slice(1, edge + 1))
                arrived = [faces[ph].at[source] for ph in range(2)]
            else:
                index = (s, slice(1, planes + 1), edge + 1 if upper else 0)
                arrived = [faces[2 + ph].at[source, first : first + planes] for ph in range(2)]
            copies = [
                pltpu.make_async_copy(arrived[ph], vol.at[index], sems.at[s * 4 + f])
                for ph in range(2)
            ]
            phase = (lax.axis_index(("mx", "my")[axis]) + upper + 1) % 2
            found.append((link < slots, phase, copies, index))
    return found


def start_halos(found, vol):
    for valid, phase, copies, index in found:
        for ph in range(2):
            @pl.when(valid & (phase == ph))
            def _(copy=copies[ph]):
                copy.start()

        @pl.when(jnp.logical_not(valid))
        def _(index=index):
            vol[index] = jnp.zeros(vol.at[index].shape, vol.dtype)


def wait_halos(found):
    for valid, _, copies, _ in found:
        @pl.when(valid)
        def _(copy=copies[0]):
            copy.wait()


def shifted(vol, s, x0, planes, dx, dy):
    edge = vol.shape[2] - 2
    view = vol[s, pl.ds(x0 + 1 + dx, planes), 1 + dy : 1 + dy + edge]
    return view.reshape(planes * edge * edge, vol.shape[4])


def z_shifted(meta, vol, zbuf, s, x0, planes):
    slots, edge, channels = vol.shape[0], vol.shape[2] - 2, vol.shape[4]
    rows = planes * edge * edge

    def beyond(face, part):
        link = meta[s * 6 + face]
        other = vol[jnp.minimum(link, slots - 1), pl.ds(x0 + 1, planes), 1 : 1 + edge]
        other = other.astype(F32).reshape(planes * edge, edge, channels)[:, part]
        return jnp.where(link < slots, other, 0.0)

    centre = shifted(vol, s, x0, planes, 0, 0)
    zbuf[:, 0:8] = beyond(4, slice(edge - 8, edge))
    zbuf[:, 8 : 8 + edge] = centre.astype(F32).reshape(planes * edge, edge, channels)
    zbuf[:, 8 + edge : 16 + edge] = beyond(5, slice(0, 8))
    below = zbuf[:, 7 : 7 + edge].astype(BF).reshape(rows, channels)
    above = zbuf[:, 9 : 9 + edge].astype(BF).reshape(rows, channels)
    return below, above


def windows(meta, vol, zbuf, s, x0, planes, direction):
    below, above = z_shifted(meta, vol, zbuf, s, x0, planes)
    d = direction
    pieces = [
        shifted(vol, s, x0, planes, dx, dy)
        for dx, dy in ((0, 0), (-d, 0), (d, 0), (0, -d), (0, d))
    ]
    pieces += [below, above] if d > 0 else [above, below]
    return jnp.concatenate(pieces, axis=1)


def add_weight_terms(acc, turned, vol, zlow, zhigh, s, x0, planes):
    channels = vol.shape[4]
    near = [(0, 0), (-1, 0), (1, 0), (0, -1), (0, 1)]
    pieces = [lambda d=d: shifted(vol, s, x0, planes, *d) for d in near]
    pieces += [lambda: zlow[...], lambda: zhigh[...]]
    left = turned[...]
    for t in range(0, len(pieces), 2):
        right = jnp.concatenate([piece() for piece in pieces[t : t + 2]], axis=1)
        at = slice(t * channels, t * channels + right.shape[1])
        acc[:, at] += jnp.dot(left, right, preferred_element_type=F32)


def pick_kernel(feat, x0, x1, y0, y1, sems):
    edge = feat.shape[1]
    copies = []
    for i, out in enumerate((x0, x1, y0, y1)):
        upward = lax.axis_index(("mx", "my")[i // 2]) % 2 == i % 2
        layer = jnp.where(upward, edge - 1, 0)
        face = feat.at[:, layer] if i < 2 else feat.at[:, :, layer]
        copies.append(pltpu.make_async_copy(face, out, sems.at[i]))
    for copy in copies:
        copy.start()
    for copy in copies:
        copy.wait()


def finish_kernel(own, other, conv_o, bias_o, head_o):
    half = own.shape[0]
    edges = (conv_o.shape[0], conv_o.shape[0] + head_o.shape[0])

    def place(h, value):
        lo = h * half
        n = min(max(edges[0] - lo, 0), half)
        if n:
            conv_o[lo : lo + n] = value[:n]
        start, stop = max(edges[0] - lo, 0), min(edges[1] - lo, half)
        if start < stop:
            at = lo + start - edges[0]
            head_o[at : at + stop - start] = value[start:stop]
        if 0 <= edges[1] - lo < half:
            bias_o[...] = value[edges[1] - lo : edges[1] - lo + 1]

    first = lax.axis_index("region") == 0
    place(0, jnp.where(first, own[...], other[...]).astype(F32))
    place(1, jnp.where(first, other[...], own[...]).astype(F32))


def forward_kernel(
    total, meta, feat, x0f, x1f, y0f, y1f, w, bias, hw, gout, ghead,
    res_o, head_o, gpre_o, gx0_o, gx1_o, gy0_o, gy1_o, colg_o, pay_o,
    vol, zbuf, colsum, acc, turned, zlow, zhigh, sems,
):
    slots, edge, channels = feat.shape[0], feat.shape[1], feat.shape[4]
    s, xi = pl.program_id(0), pl.program_id(1)
    planes = res_o.shape[1]
    steps = edge // planes
    count = total[0]
    scale = 1.0 / (edge * count).astype(F32)
    taps = w.shape[0] // channels

    @pl.when((s == 0) & (xi == 0))
    def _():
        body = [
            pltpu.make_async_copy(
                feat.at[i], vol.at[i, 1 : edge + 1, 1 : edge + 1], sems.at[slots * 4 + i]
            )
            for i in range(slots)
        ]
        found = halo_copies(meta, slots, (x0f, x1f, y0f, y1f), vol, sems, 0, edge, edge)
        for copy in body:
            copy.start()
        start_halos(found, vol)
        colg_o[...] = (
            lax.dot_general(
                ghead[...], hw[...], (((1,), (1,)), ((), ())), preferred_element_type=F32
            )
            * scale
        )
        pay_o[...] = jnp.zeros_like(pay_o)
        for ref in (acc, turned, zlow, zhigh):
            ref[...] = jnp.zeros_like(ref)
        colsum[...] = jnp.zeros_like(colsum)
        for copy in body:
            copy.wait()
        wait_halos(found)

    x0 = xi * planes
    rows = planes * edge * edge
    cols = planes * edge
    before_s = jnp.maximum(jnp.where(xi == 0, s - 1, s), 0)
    before_x0 = jnp.where(xi == 0, edge - planes, x0 - planes)
    add_weight_terms(acc, turned, vol, zlow, zhigh, before_s, before_x0, planes)
    stacked = windows(meta, vol, zbuf, s, x0, planes, 1)
    preact = jnp.dot(stacked, w[...], preferred_element_type=F32) + bias[...]
    occupied = s < count
    sigma = 0.5 * jnp.tanh(0.5 * preact) + 0.5
    silu = preact * sigma
    result = jnp.where(occupied, stacked[:, :channels].astype(F32) + silu, 0.0).astype(BF)
    res_o[0] = result.reshape(planes, edge, edge, channels)
    column = pl.ds(pl.multiple_of(x0 * edge, cols), cols)
    spread = colg_o[column].reshape(cols, 1, channels)
    grad_result = gout[0].astype(F32).reshape(cols, edge, channels) + spread
    slope = sigma * (1.0 + (preact - silu))
    gpre = jnp.where(occupied, grad_result.reshape(rows, channels) * slope, 0.0).astype(BF)
    gtile = gpre.reshape(planes, edge, edge, channels)
    gpre_o[0] = gtile
    for upper, step, layer in ((0, 0, 0), (1, steps - 1, planes - 1)):
        for phase, out in ((0, gx0_o), (1, gx1_o)):
            @pl.when((xi == step) & ((lax.axis_index("mx") % 2 == phase) == bool(upper)))
            def _(out=out, layer=layer):
                out[s] = gtile[layer]

    even = lax.axis_index("my") % 2 == 0
    low, high = gtile[:, 0], gtile[:, edge - 1]
    gy0_o[s, pl.ds(x0, planes)] = jnp.where(even, high, low)
    gy1_o[s, pl.ds(x0, planes)] = jnp.where(even, low, high)

    of_row = lax.broadcasted_iota(jnp.int32, (cols, rows), 1) // edge
    pool = (of_row == lax.broadcasted_iota(jnp.int32, (cols, rows), 0)).astype(BF)
    colsum[column] += jnp.dot(pool, result, preferred_element_type=F32)
    tail = (taps + 1) * channels
    pay_o[tail : tail + 1] += jnp.sum(gpre.astype(F32), axis=0, keepdims=True)
    turned[...] = gpre.T
    zlow[...] = stacked[:, 5 * channels : 6 * channels]
    zhigh[...] = stacked[:, 6 * channels : 7 * channels]

    @pl.when((s == slots - 1) & (xi == steps - 1))
    def _():
        add_weight_terms(acc, turned, vol, zlow, zhigh, s, x0, planes)
        for t in range(taps):
            at = slice(t * channels, (t + 1) * channels)
            pay_o[at] = acc[:, at].T
        column_bf = (colsum[...] * scale).astype(BF)
        head_o[...] = jnp.dot(column_bf, hw[...], preferred_element_type=F32).astype(BF)
        pay_o[taps * channels : tail] = lax.dot_general(
            column_bf, ghead[...], (((0,), (0,)), ((), ())), preferred_element_type=F32
        )


def backward_kernel(first, total, meta, grad, x0f, x1f, y0f, y1f, wt, gout, colg, *rest):
    out_o, vol, zbuf, sems = rest[-4:]
    slots, edge, channels = grad.shape[0], grad.shape[1], grad.shape[4]
    planes, held = gout.shape[1], vol.shape[1] - 2
    s, xi = pl.program_id(0), pl.program_id(1)

    @pl.when((s == 0) & (xi == 0))
    def _():
        below, above = min(first, 1), min(edge - first - held, 1)
        body = [
            pltpu.make_async_copy(
                grad.at[i, first - below : first + held + above],
                vol.at[i, 1 - below : 1 + held + above, 1 : edge + 1],
                sems.at[slots * 4 + i],
            )
            for i in range(slots)
        ]
        found = halo_copies(meta, slots, (x0f, x1f, y0f, y1f), vol, sems, first, held, edge)
        for copy in body:
            copy.start()
        start_halos(found, vol)
        for copy in body:
            copy.wait()
        wait_halos(found)

    rows = planes * edge * edge
    cols = planes * edge
    stacked = windows(meta, vol, zbuf, s, xi * planes, planes, -1)
    conv = jnp.dot(stacked, wt[...], preferred_element_type=F32)
    column = pl.ds(pl.multiple_of(first * edge + xi * cols, cols), cols)
    spread = colg[column].reshape(cols, 1, channels)
    grad_result = gout[0].astype(F32).reshape(cols, edge, channels) + spread
    total = jnp.where(s < total[0], grad_result.reshape(rows, channels) + conv, 0.0).astype(BF)
    out_o[0] = total.reshape(planes, edge, edge, channels)


def in_hbm(x):
    return pltpu.with_memory_space_constraint(x, pltpu.HBM)


def swap(x, axis, odd):
    pairs = []
    for i in range(odd, lax.axis_size(axis) - 1, 2):
        pairs += [(i, i + 1), (i + 1, i)]
    return lax.ppermute(x, axis, pairs)


def swap_faces(sent, axis):
    arrived = []
    for odd in range(2):
        arrived.append(swap(sent[odd], axis, odd))
    return arrived


def partner(x, axis, bit):
    return lax.ppermute(x, axis, [(i, i ^ (1 << bit)) for i in range(lax.axis_size(axis))])


def own_bit(axis, bit):
    return (lax.axis_index(axis) >> bit) & 1


def halved(x, axis, bit):
    me = own_bit(axis, bit)
    parts = x.reshape((2, x.shape[0] // 2) + x.shape[1:])
    own = lax.dynamic_index_in_dim(parts, me, 0, False)
    sent = lax.dynamic_index_in_dim(parts, 1 - me, 0, False)
    return own + partner(sent.astype(BF), axis, bit).astype(F32)


def summed(x, axis, bit):
    return x + partner(x.astype(BF), axis, bit).astype(F32)


def bits(axis):
    return range((lax.axis_size(axis) - 1).bit_length())


def all_summed(x):
    x = halved(x, "region", 0)
    later = [(axis, b) for axis in ("mx", "my") for b in bits(axis) if b]
    for axis, bit in [("my", 0), ("mx", 0)] + sorted(later, key=lambda stage: stage[1]):
        x = summed(x, axis, bit)
    x = x.astype(BF)
    return x, partner(x, "region", 0)


def body(
    features_in, conv_weight, conv_bias, head_weight, grad_out, grad_head, block_count, neighbours
):
    blocks = features_in.reshape(features_in.shape[3:])
    upstream = grad_out.reshape(grad_out.shape[3:])
    head_grad = grad_head.reshape(grad_head.shape[3:])
    slots, edge, channels = blocks.shape[0], blocks.shape[1], blocks.shape[4]
    taps = conv_weight.shape[0]
    meta = (block_count.reshape(1), neighbours.reshape(-1))
    anywhere = pl.BlockSpec(memory_space=pl.ANY)
    hbm = pl.BlockSpec(memory_space=pltpu.HBM)
    vmem = pl.BlockSpec(memory_space=pltpu.VMEM)
    face = jax.ShapeDtypeStruct((slots, edge, edge, channels), BF)
    sent = pl.pallas_call(
        pick_kernel,
        in_specs=[hbm],
        out_specs=[vmem] * 4,
        scratch_shapes=[pltpu.SemaphoreType.DMA((4,))],
        out_shape=[face] * 4,
        compiler_params=pltpu.CompilerParams(vmem_limit_bytes=8 << 20),
        name="pick",
    )(in_hbm(blocks))
    faces = swap_faces(sent[:2], "mx") + swap_faces(sent[2:], "my")

    whole = lambda *shape: pl.BlockSpec(shape, lambda i, j, m, n: (0,) * len(shape))
    tile = pl.BlockSpec((1, PLANES, edge, edge, channels), lambda i, j, m, n: (i, j, 0, 0, 0))
    volume = (slots, edge, edge, edge, channels)
    padded = pltpu.VMEM((slots, edge + 2, edge + 2, edge, channels), BF)
    columns = edge * edge
    pay_rows = ((taps + 1) * channels // 32 + 1) * 32
    flops = 2 * slots * edge**3 * taps * channels * channels
    moved = slots * edge**3 * channels * 2
    params = pltpu.CompilerParams(
        dimension_semantics=("arbitrary", "arbitrary"), vmem_limit_bytes=GRANT
    )
    result, head_tile, gpre, gx0, gx1, gy0, gy1, colg, pay = pl.pallas_call(
        forward_kernel,
        grid_spec=pltpu.PrefetchScalarGridSpec(
            num_scalar_prefetch=2,
            grid=(slots, edge // PLANES),
            in_specs=[
                hbm, anywhere, anywhere, anywhere, anywhere,
                whole(taps * channels, channels), whole(1, channels), whole(channels, channels),
                tile, whole(columns, channels),
            ],
            out_specs=[
                tile, whole(columns, channels), tile,
                *[whole(slots, edge, edge, channels)] * 4,
                whole(columns, channels), whole(pay_rows, channels),
            ],
            scratch_shapes=[
                padded, pltpu.VMEM((PLANES * edge, edge + 16, channels), F32),
                pltpu.VMEM((columns, channels), F32),
                pltpu.VMEM((channels, taps * channels), F32),
                pltpu.VMEM((channels, PLANES * columns), BF),
                pltpu.VMEM((PLANES * columns, channels), BF),
                pltpu.VMEM((PLANES * columns, channels), BF),
                pltpu.SemaphoreType.DMA((slots * 5,)),
            ],
        ),
        out_shape=[
            pltpu.HBM(volume, BF),
            jax.ShapeDtypeStruct((columns, channels), BF),
            pltpu.HBM(volume, BF),
            *[face] * 4,
            jax.ShapeDtypeStruct((columns, channels), F32),
            jax.ShapeDtypeStruct((pay_rows, channels), F32),
        ],
        compiler_params=params,
        cost_estimate=pl.CostEstimate(
            flops=2 * flops, bytes_accessed=5 * moved, transcendentals=moved // 2
        ),
        name="forward",
    )(
        *meta, in_hbm(blocks), *faces, in_hbm(conv_weight.reshape(taps * channels, channels)),
        conv_bias.reshape(1, channels), in_hbm(head_weight), in_hbm(upstream), in_hbm(head_grad),
    )

    grad_faces = swap_faces((gx0, gx1), "mx") + swap_faces((gy0, gy1), "my")
    turned = jnp.transpose(conv_weight, (0, 2, 1)).reshape(taps * channels, channels)
    grad_local = None
    pieces = edge // PIECE
    for k in range(pieces):
        part = pl.BlockSpec(
            (1, STEP, edge, edge, channels),
            lambda i, j, m, n, k=k: (i, k * (PIECE // STEP) + j, 0, 0, 0),
        )
        all_of = lambda *shape: pl.BlockSpec(shape, lambda i, j, m, n: (0,) * len(shape))
        operands = [*meta, in_hbm(gpre), *grad_faces, turned, in_hbm(upstream), colg]
        specs = [hbm] + [anywhere] * 4
        specs += [all_of(taps * channels, channels), part, all_of(columns, channels)]
        if grad_local is not None:
            operands.append(grad_local)
            specs.append(hbm)
        grad_local = pl.pallas_call(
            functools.partial(backward_kernel, k * PIECE),
            grid_spec=pltpu.PrefetchScalarGridSpec(
                num_scalar_prefetch=2,
                grid=(slots, PIECE // STEP),
                in_specs=specs,
                out_specs=part,
                scratch_shapes=[
                    pltpu.VMEM((slots, PIECE + 2, edge + 2, edge, channels), BF),
                    pltpu.VMEM((STEP * edge, edge + 16, channels), F32),
                    pltpu.SemaphoreType.DMA((slots * 5,)),
                ],
            ),
            out_shape=jax.ShapeDtypeStruct(volume, BF),
            input_output_aliases={len(operands) - 1: 0} if k else {},
            compiler_params=pltpu.CompilerParams(
                dimension_semantics=("arbitrary", "arbitrary"), vmem_limit_bytes=GRANT
            ),
            cost_estimate=pl.CostEstimate(
                flops=flops // pieces, bytes_accessed=4 * moved // pieces, transcendentals=0
            ),
        )(*operands)

    own, other = all_summed(pay)
    conv_rows = taps * channels
    grad_conv, grad_bias, grad_head_weight = pl.pallas_call(
        finish_kernel,
        in_specs=[vmem] * 2,
        out_specs=[vmem] * 3,
        out_shape=[
            jax.ShapeDtypeStruct((conv_rows, channels), F32),
            jax.ShapeDtypeStruct((1, channels), F32),
            jax.ShapeDtypeStruct((channels, channels), F32),
        ],
        compiler_params=pltpu.CompilerParams(vmem_limit_bytes=8 << 20),
        name="finish",
    )(own, other)
    return (
        result.reshape(features_in.shape),
        head_tile.reshape(grad_head.shape),
        grad_local.reshape(features_in.shape),
        grad_conv.reshape(conv_weight.shape),
        grad_bias.reshape(channels),
        grad_head_weight,
    )


def solution(mesh):
    tiles = P("region", "mx", "my", None, None, None, None, None)
    rows = P("region", "mx", "my", None, None)

    return jax.shard_map(
        body,
        mesh=mesh,
        in_specs=(tiles, P(), P(), P(), tiles, rows, P("region", "mx", "my"), rows),
        out_specs=(tiles, rows, tiles, P(), P(), P()),
        check_vma=False,
    )
```

```python
import functools

import jax
import jax.numpy as jnp
from jax import lax
from jax.experimental import pallas as pl
from jax.experimental.pallas import tpu as pltpu
from jax.sharding import PartitionSpec as P


BF = jnp.bfloat16
F32 = jnp.float32
PLANES = 8
PIECE = 16
STEP = 8
GRANT = 44 << 20


def halo_copies(meta, slots, faces, vol, sems, first, planes, edge, paired):
    found = []
    for s in range(slots):
        for f in range(4):
            link = meta[s * 6 + f]
            axis, upper = f // 2, f % 2
            if axis == 0 and first + (planes if upper else 0) != (edge if upper else 0):
                continue
            source = jnp.minimum(link, slots - 1)
            if axis == 0:
                index = (s, planes + 1 if upper else 0, slice(1, edge + 1))
                part = ()
            else:
                index = (s, slice(1, planes + 1), edge + 1 if upper else 0)
                part = (slice(first, first + planes),)
            valid = link < slots
            if paired:
                phase = (lax.axis_index(("mx", "my")[axis]) + upper + 1) % 2
                wanted = [(valid & (phase == ph), faces[2 * axis + ph]) for ph in range(2)]
            else:
                wanted = [(valid, faces[f])]
            copies = [
                (
                    condition,
                    pltpu.make_async_copy(face.at[(source,) + part], vol.at[index], sems.at[s * 4 + f]),
                )
                for condition, face in wanted
            ]
            found.append((valid, copies, index))
    return found


def start_halos(found, vol):
    for valid, copies, index in found:
        for wanted, copy in copies:
            @pl.when(wanted)
            def _(copy=copy):
                copy.start()

        @pl.when(jnp.logical_not(valid))
        def _(index=index):
            vol[index] = jnp.zeros(vol.at[index].shape, vol.dtype)


def wait_halos(found):
    for valid, copies, _ in found:
        @pl.when(valid)
        def _(copy=copies[0][1]):
            copy.wait()


def shifted(vol, s, x0, planes, dx, dy):
    edge = vol.shape[2] - 2
    view = vol[s, pl.ds(x0 + 1 + dx, planes), 1 + dy : 1 + dy + edge]
    return view.reshape(planes * edge * edge, vol.shape[4])


def z_shifted(meta, vol, zbuf, s, x0, planes):
    slots, edge, channels = vol.shape[0], vol.shape[2] - 2, vol.shape[4]
    rows = planes * edge * edge

    def beyond(face, part):
        link = meta[s * 6 + face]
        other = vol[jnp.minimum(link, slots - 1), pl.ds(x0 + 1, planes), 1 : 1 + edge]
        other = other.astype(F32).reshape(planes * edge, edge, channels)[:, part]
        return jnp.where(link < slots, other, 0.0)

    centre = shifted(vol, s, x0, planes, 0, 0)
    zbuf[:, 0:8] = beyond(4, slice(edge - 8, edge))
    zbuf[:, 8 : 8 + edge] = centre.astype(F32).reshape(planes * edge, edge, channels)
    zbuf[:, 8 + edge : 16 + edge] = beyond(5, slice(0, 8))
    below = zbuf[:, 7 : 7 + edge].astype(BF).reshape(rows, channels)
    above = zbuf[:, 9 : 9 + edge].astype(BF).reshape(rows, channels)
    return below, above


def windows(meta, vol, zbuf, s, x0, planes, direction):
    below, above = z_shifted(meta, vol, zbuf, s, x0, planes)
    d = direction
    pieces = [
        shifted(vol, s, x0, planes, dx, dy)
        for dx, dy in ((0, 0), (-d, 0), (d, 0), (0, -d), (0, d))
    ]
    pieces += [below, above] if d > 0 else [above, below]
    return jnp.concatenate(pieces, axis=1)


def add_weight_terms(acc, turned, vol, zlow, zhigh, s, x0, planes):
    channels = vol.shape[4]
    near = [(0, 0), (-1, 0), (1, 0), (0, -1), (0, 1)]
    pieces = [lambda d=d: shifted(vol, s, x0, planes, *d) for d in near]
    pieces += [lambda: zlow[...], lambda: zhigh[...]]
    left = turned[...]
    for t in range(0, len(pieces), 2):
        right = jnp.concatenate([piece() for piece in pieces[t : t + 2]], axis=1)
        at = slice(t * channels, t * channels + right.shape[1])
        acc[:, at] += jnp.dot(left, right, preferred_element_type=F32)


def pick_kernel(feat, x0, x1, y0, y1, sems):
    edge = feat.shape[1]
    copies = []
    for i, out in enumerate((x0, x1, y0, y1)):
        layer = 0 if i % 2 else edge - 1
        face = feat.at[:, layer] if i < 2 else feat.at[:, :, layer]
        copies.append(pltpu.make_async_copy(face, out, sems.at[i]))
    for copy in copies:
        copy.start()
    for copy in copies:
        copy.wait()


def finish_kernel(own, other, conv_o, bias_o, head_o):
    half = own.shape[0]
    edges = (conv_o.shape[0], conv_o.shape[0] + head_o.shape[0])

    def place(h, value):
        lo = h * half
        n = min(max(edges[0] - lo, 0), half)
        if n:
            conv_o[lo : lo + n] = value[:n]
        start, stop = max(edges[0] - lo, 0), min(edges[1] - lo, half)
        if start < stop:
            at = lo + start - edges[0]
            head_o[at : at + stop - start] = value[start:stop]
        if 0 <= edges[1] - lo < half:
            bias_o[...] = value[edges[1] - lo : edges[1] - lo + 1]

    first = lax.axis_index("region") == 0
    place(0, jnp.where(first, own[...], other[...]).astype(F32))
    place(1, jnp.where(first, other[...], own[...]).astype(F32))


def forward_kernel(
    total, meta, feat, x0f, x1f, y0f, y1f, w, bias, hw, gout, ghead,
    res_o, head_o, gpre_o, gx0_o, gx1_o, gy0_o, gy1_o, colg_o, pay_o,
    vol, zbuf, colsum, acc, turned, zlow, zhigh, sems,
):
    slots, edge, channels = feat.shape[0], feat.shape[1], feat.shape[4]
    s, xi = pl.program_id(0), pl.program_id(1)
    planes = res_o.shape[1]
    steps = edge // planes
    count = total[0]
    scale = 1.0 / (edge * count).astype(F32)
    taps = w.shape[0] // channels

    cut = min(planes + 1, edge)
    parts = [
        [
            pltpu.make_async_copy(
                feat.at[i, lo:hi],
                vol.at[i, 1 + lo : 1 + hi, 1 : edge + 1],
                sems.at[slots * (4 + h) + i],
            )
            for i in range(slots)
        ]
        for h, (lo, hi) in enumerate(((0, cut), (cut, edge)))
    ]

    @pl.when((s == 0) & (xi == 0))
    def _():
        body = parts[0] + parts[1]
        found = halo_copies(meta, slots, (x0f, x1f, y0f, y1f), vol, sems, 0, edge, edge, False)
        for copy in body:
            copy.start()
        start_halos(found, vol)
        colg_o[...] = (
            lax.dot_general(
                ghead[...], hw[...], (((1,), (1,)), ((), ())), preferred_element_type=F32
            )
            * scale
        )
        pay_o[...] = jnp.zeros_like(pay_o)
        for ref in (acc, turned, zlow, zhigh):
            ref[...] = jnp.zeros_like(ref)
        colsum[...] = jnp.zeros_like(colsum)
        for copy in parts[0]:
            copy.wait()
        wait_halos(found)

    @pl.when((s == 0) & (xi == 1))
    def _():
        for copy in parts[1]:
            copy.wait()

    x0 = xi * planes
    rows = planes * edge * edge
    cols = planes * edge
    before_s = jnp.maximum(jnp.where(xi == 0, s - 1, s), 0)
    before_x0 = jnp.where(xi == 0, jnp.where(s == 0, 0, edge - planes), x0 - planes)
    add_weight_terms(acc, turned, vol, zlow, zhigh, before_s, before_x0, planes)
    stacked = windows(meta, vol, zbuf, s, x0, planes, 1)
    preact = jnp.dot(stacked, w[...], preferred_element_type=F32) + bias[...]
    occupied = s < count
    sigma = 0.5 * jnp.tanh(0.5 * preact) + 0.5
    silu = preact * sigma
    result = jnp.where(occupied, stacked[:, :channels].astype(F32) + silu, 0.0).astype(BF)
    res_o[0] = result.reshape(planes, edge, edge, channels)
    column = pl.ds(pl.multiple_of(x0 * edge, cols), cols)
    spread = colg_o[column].reshape(cols, 1, channels)
    grad_result = gout[0].astype(F32).reshape(cols, edge, channels) + spread
    slope = sigma * (1.0 + (preact - silu))
    gpre = jnp.where(occupied, grad_result.reshape(rows, channels) * slope, 0.0).astype(BF)
    gtile = gpre.reshape(planes, edge, edge, channels)
    gpre_o[0] = gtile
    for upper, step, layer in ((0, 0, 0), (1, steps - 1, planes - 1)):
        for phase, out in ((0, gx0_o), (1, gx1_o)):
            @pl.when((xi == step) & ((lax.axis_index("mx") % 2 == phase) == bool(upper)))
            def _(out=out, layer=layer):
                out[s] = gtile[layer]

    even = lax.axis_index("my") % 2 == 0
    low, high = gtile[:, 0], gtile[:, edge - 1]
    gy0_o[s, pl.ds(x0, planes)] = jnp.where(even, high, low)
    gy1_o[s, pl.ds(x0, planes)] = jnp.where(even, low, high)

    of_row = lax.broadcasted_iota(jnp.int32, (cols, rows), 1) // edge
    pool = (of_row == lax.broadcasted_iota(jnp.int32, (cols, rows), 0)).astype(BF)
    colsum[column] += jnp.dot(pool, result, preferred_element_type=F32)
    tail = (taps + 1) * channels
    pay_o[tail : tail + 1] += jnp.sum(gpre.astype(F32), axis=0, keepdims=True)
    turned[...] = gpre.T
    zlow[...] = stacked[:, 5 * channels : 6 * channels]
    zhigh[...] = stacked[:, 6 * channels : 7 * channels]

    @pl.when((s == slots - 1) & (xi == steps - 1))
    def _():
        add_weight_terms(acc, turned, vol, zlow, zhigh, s, x0, planes)
        for t in range(taps):
            at = slice(t * channels, (t + 1) * channels)
            pay_o[at] = acc[:, at].T
        column_bf = (colsum[...] * scale).astype(BF)
        head_o[...] = jnp.dot(column_bf, hw[...], preferred_element_type=F32).astype(BF)
        pay_o[taps * channels : tail] = lax.dot_general(
            column_bf, ghead[...], (((0,), (0,)), ((), ())), preferred_element_type=F32
        )


def backward_kernel(first, total, meta, grad, x0f, x1f, y0f, y1f, wt, gout, colg, *rest):
    out_o, vol, zbuf, sems = rest[-4:]
    slots, edge, channels = grad.shape[0], grad.shape[1], grad.shape[4]
    planes, held = gout.shape[1], vol.shape[1] - 2
    s, xi = pl.program_id(0), pl.program_id(1)

    below, above = min(first, 1), min(edge - first - held, 1)
    cut = min(planes + 1, held)
    parts = [
        [
            pltpu.make_async_copy(
                grad.at[i, first + lo : first + hi],
                vol.at[i, 1 + lo : 1 + hi, 1 : edge + 1],
                sems.at[slots * (4 + h) + i],
            )
            for i in range(slots)
        ]
        for h, (lo, hi) in enumerate(((-below, cut), (cut, held + above)))
    ]

    @pl.when((s == 0) & (xi == 0))
    def _():
        body = parts[0] + parts[1]
        found = halo_copies(meta, slots, (x0f, x1f, y0f, y1f), vol, sems, first, held, edge, True)
        for copy in body:
            copy.start()
        start_halos(found, vol)
        for copy in parts[0]:
            copy.wait()
        wait_halos(found)

    @pl.when((s == 0) & (xi == 1))
    def _():
        for copy in parts[1]:
            copy.wait()

    rows = planes * edge * edge
    cols = planes * edge
    stacked = windows(meta, vol, zbuf, s, xi * planes, planes, -1)
    conv = jnp.dot(stacked, wt[...], preferred_element_type=F32)
    column = pl.ds(pl.multiple_of(first * edge + xi * cols, cols), cols)
    spread = colg[column].reshape(cols, 1, channels)
    grad_result = gout[0].astype(F32).reshape(cols, edge, channels) + spread
    total = jnp.where(s < total[0], grad_result.reshape(rows, channels) + conv, 0.0).astype(BF)
    out_o[0] = total.reshape(planes, edge, edge, channels)


def in_hbm(x):
    return pltpu.with_memory_space_constraint(x, pltpu.HBM)


def swap(x, axis, odd):
    pairs = []
    for i in range(odd, lax.axis_size(axis) - 1, 2):
        pairs += [(i, i + 1), (i + 1, i)]
    return lax.ppermute(x, axis, pairs)


def swap_faces(sent, axis):
    arrived = []
    for odd in range(2):
        arrived.append(swap(sent[odd], axis, odd))
    return arrived


def turn(x, axis, by):
    count = lax.axis_size(axis)
    return lax.ppermute(x, axis, [(i, (i + by) % count) for i in range(count)])


def turn_faces(sent, axis):
    arrived = []
    for i, by in enumerate((1, -1)):
        arrived.append(turn(sent[i], axis, by))
    return arrived


def partner(x, axis, bit):
    return lax.ppermute(x, axis, [(i, i ^ (1 << bit)) for i in range(lax.axis_size(axis))])


def own_bit(axis, bit):
    return (lax.axis_index(axis) >> bit) & 1


def halved(x, axis, bit):
    me = own_bit(axis, bit)
    parts = x.reshape((2, x.shape[0] // 2) + x.shape[1:])
    own = lax.dynamic_index_in_dim(parts, me, 0, False)
    sent = lax.dynamic_index_in_dim(parts, 1 - me, 0, False)
    return own + partner(sent.astype(BF), axis, bit).astype(F32)


def summed(x, axis, bit):
    return x + partner(x.astype(BF), axis, bit).astype(F32)


def bits(axis):
    return range((lax.axis_size(axis) - 1).bit_length())


def all_summed(x):
    x = halved(x, "region", 0)
    later = [(axis, b) for axis in ("mx", "my") for b in bits(axis) if b]
    for axis, bit in [("my", 0), ("mx", 0)] + sorted(later, key=lambda stage: stage[1]):
        x = summed(x, axis, bit)
    x = x.astype(BF)
    return x, partner(x, "region", 0)


def body(
    features_in, conv_weight, conv_bias, head_weight, grad_out, grad_head, block_count, neighbours
):
    blocks = features_in.reshape(features_in.shape[3:])
    upstream = grad_out.reshape(grad_out.shape[3:])
    head_grad = grad_head.reshape(grad_head.shape[3:])
    slots, edge, channels = blocks.shape[0], blocks.shape[1], blocks.shape[4]
    taps = conv_weight.shape[0]
    meta = (block_count.reshape(1), neighbours.reshape(-1))
    anywhere = pl.BlockSpec(memory_space=pl.ANY)
    hbm = pl.BlockSpec(memory_space=pltpu.HBM)
    vmem = pl.BlockSpec(memory_space=pltpu.VMEM)
    face = jax.ShapeDtypeStruct((slots, edge, edge, channels), BF)
    sent = pl.pallas_call(
        pick_kernel,
        in_specs=[hbm],
        out_specs=[vmem] * 4,
        scratch_shapes=[pltpu.SemaphoreType.DMA((4,))],
        out_shape=[face] * 4,
        compiler_params=pltpu.CompilerParams(vmem_limit_bytes=8 << 20),
        name="pick",
    )(in_hbm(blocks))
    faces = turn_faces(sent[:2], "mx") + turn_faces(sent[2:], "my")

    whole = lambda *shape: pl.BlockSpec(shape, lambda i, j, m, n: (0,) * len(shape))
    tile = pl.BlockSpec((1, PLANES, edge, edge, channels), lambda i, j, m, n: (i, j, 0, 0, 0))
    volume = (slots, edge, edge, edge, channels)
    padded = pltpu.VMEM((slots, edge + 2, edge + 2, edge, channels), BF)
    columns = edge * edge
    pay_rows = ((taps + 1) * channels // 32 + 1) * 32
    flops = 2 * slots * edge**3 * taps * channels * channels
    moved = slots * edge**3 * channels * 2
    params = pltpu.CompilerParams(
        dimension_semantics=("arbitrary", "arbitrary"), vmem_limit_bytes=GRANT
    )
    result, head_tile, gpre, gx0, gx1, gy0, gy1, colg, pay = pl.pallas_call(
        forward_kernel,
        grid_spec=pltpu.PrefetchScalarGridSpec(
            num_scalar_prefetch=2,
            grid=(slots, edge // PLANES),
            in_specs=[
                hbm, anywhere, anywhere, anywhere, anywhere,
                whole(taps * channels, channels), whole(1, channels), whole(channels, channels),
                tile, whole(columns, channels),
            ],
            out_specs=[
                tile, whole(columns, channels), tile,
                *[whole(slots, edge, edge, channels)] * 4,
                whole(columns, channels), whole(pay_rows, channels),
            ],
            scratch_shapes=[
                padded, pltpu.VMEM((PLANES * edge, edge + 16, channels), F32),
                pltpu.VMEM((columns, channels), F32),
                pltpu.VMEM((channels, taps * channels), F32),
                pltpu.VMEM((channels, PLANES * columns), BF),
                pltpu.VMEM((PLANES * columns, channels), BF),
                pltpu.VMEM((PLANES * columns, channels), BF),
                pltpu.SemaphoreType.DMA((slots * 6,)),
            ],
        ),
        out_shape=[
            pltpu.HBM(volume, BF),
            jax.ShapeDtypeStruct((columns, channels), BF),
            pltpu.HBM(volume, BF),
            *[face] * 4,
            jax.ShapeDtypeStruct((columns, channels), F32),
            jax.ShapeDtypeStruct((pay_rows, channels), F32),
        ],
        compiler_params=params,
        cost_estimate=pl.CostEstimate(
            flops=2 * flops, bytes_accessed=5 * moved, transcendentals=moved // 2
        ),
        name="forward",
    )(
        *meta, in_hbm(blocks), *faces, in_hbm(conv_weight.reshape(taps * channels, channels)),
        conv_bias.reshape(1, channels), in_hbm(head_weight), in_hbm(upstream), in_hbm(head_grad),
    )

    grad_faces = swap_faces((gx0, gx1), "mx") + swap_faces((gy0, gy1), "my")
    turned = jnp.transpose(conv_weight, (0, 2, 1)).reshape(taps * channels, channels)
    grad_local = None
    pieces = edge // PIECE
    for k in range(pieces):
        part = pl.BlockSpec(
            (1, STEP, edge, edge, channels),
            lambda i, j, m, n, k=k: (i, k * (PIECE // STEP) + j, 0, 0, 0),
        )
        all_of = lambda *shape: pl.BlockSpec(shape, lambda i, j, m, n: (0,) * len(shape))
        operands = [*meta, in_hbm(gpre), *grad_faces, turned, in_hbm(upstream), colg]
        specs = [hbm] + [anywhere] * 4
        specs += [all_of(taps * channels, channels), part, all_of(columns, channels)]
        if grad_local is not None:
            operands.append(grad_local)
            specs.append(hbm)
        grad_local = pl.pallas_call(
            functools.partial(backward_kernel, k * PIECE),
            grid_spec=pltpu.PrefetchScalarGridSpec(
                num_scalar_prefetch=2,
                grid=(slots, PIECE // STEP),
                in_specs=specs,
                out_specs=part,
                scratch_shapes=[
                    pltpu.VMEM((slots, PIECE + 2, edge + 2, edge, channels), BF),
                    pltpu.VMEM((STEP * edge, edge + 16, channels), F32),
                    pltpu.SemaphoreType.DMA((slots * 6,)),
                ],
            ),
            out_shape=jax.ShapeDtypeStruct(volume, BF),
            input_output_aliases={len(operands) - 1: 0} if k else {},
            compiler_params=pltpu.CompilerParams(
                dimension_semantics=("arbitrary", "arbitrary"), vmem_limit_bytes=GRANT
            ),
            cost_estimate=pl.CostEstimate(
                flops=flops // pieces, bytes_accessed=4 * moved // pieces, transcendentals=0
            ),
        )(*operands)

    own, other = all_summed(pay)
    conv_rows = taps * channels
    grad_conv, grad_bias, grad_head_weight = pl.pallas_call(
        finish_kernel,
        in_specs=[vmem] * 2,
        out_specs=[vmem] * 3,
        out_shape=[
            jax.ShapeDtypeStruct((conv_rows, channels), F32),
            jax.ShapeDtypeStruct((1, channels), F32),
            jax.ShapeDtypeStruct((channels, channels), F32),
        ],
        compiler_params=pltpu.CompilerParams(vmem_limit_bytes=8 << 20),
        name="finish",
    )(own, other)
    return (
        result.reshape(features_in.shape),
        head_tile.reshape(grad_head.shape),
        grad_local.reshape(features_in.shape),
        grad_conv.reshape(conv_weight.shape),
        grad_bias.reshape(channels),
        grad_head_weight,
    )


def solution(mesh):
    tiles = P("region", "mx", "my", None, None, None, None, None)
    rows = P("region", "mx", "my", None, None)

    return jax.shard_map(
        body,
        mesh=mesh,
        in_specs=(tiles, P(), P(), P(), tiles, rows, P("region", "mx", "my"), rows),
        out_specs=(tiles, rows, tiles, P(), P(), P()),
        check_vma=False,
    )
```

```python
import functools

import jax
import jax.numpy as jnp
from jax import lax
from jax.experimental import pallas as pl
from jax.experimental.pallas import tpu as pltpu
from jax.sharding import PartitionSpec as P


BF = jnp.bfloat16
F32 = jnp.float32
PLANES = 8
PIECE = 16
STEP = 8
GRANT = 44 << 20


def halo_copies(meta, slots, faces, vol, sems, first, planes, edge, paired):
    found = []
    for s in range(slots):
        for f in range(4):
            link = meta[s * 6 + f]
            axis, upper = f // 2, f % 2
            if axis == 0 and first + (planes if upper else 0) != (edge if upper else 0):
                continue
            source = jnp.minimum(link, slots - 1)
            if axis == 0:
                index = (s, planes + 1 if upper else 0, slice(1, edge + 1))
                part = ()
            else:
                index = (s, slice(1, planes + 1), edge + 1 if upper else 0)
                part = (slice(first, first + planes),)
            valid = link < slots
            if paired:
                phase = (lax.axis_index(("mx", "my")[axis]) + upper + 1) % 2
                wanted = [(valid & (phase == ph), faces[2 * axis + ph]) for ph in range(2)]
            else:
                wanted = [(valid, faces[f])]
            copies = [
                (
                    condition,
                    pltpu.make_async_copy(face.at[(source,) + part], vol.at[index], sems.at[s * 4 + f]),
                )
                for condition, face in wanted
            ]
            found.append((valid, copies, index))
    return found


def start_halos(found, vol):
    for valid, copies, index in found:
        for wanted, copy in copies:
            @pl.when(wanted)
            def _(copy=copy):
                copy.start()

        @pl.when(jnp.logical_not(valid))
        def _(index=index):
            vol[index] = jnp.zeros(vol.at[index].shape, vol.dtype)


def wait_halos(found):
    for valid, copies, _ in found:
        @pl.when(valid)
        def _(copy=copies[0][1]):
            copy.wait()


def shifted(vol, s, x0, planes, dx, dy):
    edge = vol.shape[2] - 2
    view = vol[s, pl.ds(x0 + 1 + dx, planes), 1 + dy : 1 + dy + edge]
    return view.reshape(planes * edge * edge, vol.shape[4])


def z_shifted(meta, vol, zbuf, s, x0, planes):
    slots, edge, channels = vol.shape[0], vol.shape[2] - 2, vol.shape[4]
    rows = planes * edge * edge

    def beyond(face, part):
        link = meta[s * 6 + face]
        other = vol[jnp.minimum(link, slots - 1), pl.ds(x0 + 1, planes), 1 : 1 + edge]
        other = other.astype(F32).reshape(planes * edge, edge, channels)[:, part]
        return jnp.where(link < slots, other, 0.0)

    centre = shifted(vol, s, x0, planes, 0, 0)
    zbuf[:, 0:8] = beyond(4, slice(edge - 8, edge))
    zbuf[:, 8 : 8 + edge] = centre.astype(F32).reshape(planes * edge, edge, channels)
    zbuf[:, 8 + edge : 16 + edge] = beyond(5, slice(0, 8))
    below = zbuf[:, 7 : 7 + edge].astype(BF).reshape(rows, channels)
    above = zbuf[:, 9 : 9 + edge].astype(BF).reshape(rows, channels)
    return below, above


def windows(meta, vol, zbuf, s, x0, planes, direction):
    below, above = z_shifted(meta, vol, zbuf, s, x0, planes)
    d = direction
    pieces = [
        shifted(vol, s, x0, planes, dx, dy)
        for dx, dy in ((0, 0), (-d, 0), (d, 0), (0, -d), (0, d))
    ]
    pieces += [below, above] if d > 0 else [above, below]
    return jnp.concatenate(pieces, axis=1)


def add_weight_terms(acc, turned, vol, zlow, zhigh, s, x0, planes):
    channels = vol.shape[4]
    near = [(0, 0), (-1, 0), (1, 0), (0, -1), (0, 1)]
    pieces = [lambda d=d: shifted(vol, s, x0, planes, *d) for d in near]
    pieces += [lambda: zlow[...], lambda: zhigh[...]]
    left = turned[...]
    for t in range(0, len(pieces), 2):
        right = jnp.concatenate([piece() for piece in pieces[t : t + 2]], axis=1)
        at = slice(t * channels, t * channels + right.shape[1])
        acc[:, at] += jnp.dot(left, right, preferred_element_type=F32)


def pick_kernel(feat, x0, x1, y0, y1, sems):
    edge = feat.shape[1]
    copies = []
    for i, out in enumerate((x0, x1, y0, y1)):
        layer = 0 if i % 2 else edge - 1
        face = feat.at[:, layer] if i < 2 else feat.at[:, :, layer]
        copies.append(pltpu.make_async_copy(face, out, sems.at[i]))
    for copy in copies:
        copy.start()
    for copy in copies:
        copy.wait()


def finish_kernel(own, other, conv_o, bias_o, head_o):
    half = own.shape[0]
    edges = (conv_o.shape[0], conv_o.shape[0] + head_o.shape[0])

    def place(h, value):
        lo = h * half
        n = min(max(edges[0] - lo, 0), half)
        if n:
            conv_o[lo : lo + n] = value[:n]
        start, stop = max(edges[0] - lo, 0), min(edges[1] - lo, half)
        if start < stop:
            at = lo + start - edges[0]
            head_o[at : at + stop - start] = value[start:stop]
        if 0 <= edges[1] - lo < half:
            bias_o[...] = value[edges[1] - lo : edges[1] - lo + 1]

    first = lax.axis_index("region") == 0
    place(0, jnp.where(first, own[...], other[...]).astype(F32))
    place(1, jnp.where(first, other[...], own[...]).astype(F32))


def forward_kernel(
    total, meta, feat, x0f, x1f, y0f, y1f, w_in, bias_in, hw_in, gout_in, ghead_in,
    res_o, head_o, gpre_o, gx0_o, gx1_o, gy0_o, gy1_o, colg_o, pay_o,
    vol, zbuf, colsum, acc, turned, zlow, zhigh, w, bias, hw, ghead, gout, sems, loads,
):
    slots, edge, channels = feat.shape[0], feat.shape[1], feat.shape[4]
    s, xi = pl.program_id(0), pl.program_id(1)
    planes = res_o.shape[1]
    steps = edge // planes
    count = total[0]
    scale = 1.0 / (edge * count).astype(F32)
    taps = w.shape[0] // channels

    small = [
        pltpu.make_async_copy(source, target, loads.at[i])
        for i, (source, target) in enumerate(
            ((ghead_in, ghead), (hw_in, hw), (w_in, w), (bias_in, bias))
        )
    ]

    def upstream(of_slot, step):
        at = (of_slot, pl.ds(step * planes, planes))
        return pltpu.make_async_copy(
            gout_in.at[at], gout.at[at], loads.at[4 + of_slot * steps + step]
        )

    cut = min(planes + 1, edge)
    parts = [
        [
            pltpu.make_async_copy(
                feat.at[i, lo:hi],
                vol.at[i, 1 + lo : 1 + hi, 1 : edge + 1],
                sems.at[slots * (4 + h) + i],
            )
            for i in range(slots)
        ]
        for h, (lo, hi) in enumerate(((0, cut), (cut, edge)))
    ]

    @pl.when((s == 0) & (xi == 0))
    def _():
        found = halo_copies(meta, slots, (x0f, x1f, y0f, y1f), vol, sems, 0, edge, edge, False)
        for copy in small[:2] + parts[0]:
            copy.start()
        start_halos(found, vol)
        for copy in small[2:]:
            copy.start()
        upstream(0, 0).start()
        for copy in parts[1]:
            copy.start()
        for of_slot in range(slots):
            for step in range(steps):
                if (of_slot, step) != (0, 0):
                    upstream(of_slot, step).start()
        pay_o[...] = jnp.zeros_like(pay_o)
        for ref in (acc, turned, zlow, zhigh):
            ref[...] = jnp.zeros_like(ref)
        colsum[...] = jnp.zeros_like(colsum)
        for copy in small[:2]:
            copy.wait()
        colg_o[...] = (
            lax.dot_general(
                ghead[...], hw[...], (((1,), (1,)), ((), ())), preferred_element_type=F32
            )
            * scale
        )
        for copy in parts[0] + small[2:]:
            copy.wait()
        wait_halos(found)

    @pl.when((s == 0) & (xi == 1))
    def _():
        for copy in parts[1]:
            copy.wait()

    upstream(s, xi).wait()
    x0 = xi * planes
    rows = planes * edge * edge
    cols = planes * edge
    before_s = jnp.maximum(jnp.where(xi == 0, s - 1, s), 0)
    before_x0 = jnp.where(xi == 0, jnp.where(s == 0, 0, edge - planes), x0 - planes)
    stacked = windows(meta, vol, zbuf, s, x0, planes, 1)
    preact = jnp.dot(stacked, w[...], preferred_element_type=F32) + bias[...]
    add_weight_terms(acc, turned, vol, zlow, zhigh, before_s, before_x0, planes)
    occupied = s < count
    sigma = 0.5 * jnp.tanh(0.5 * preact) + 0.5
    silu = preact * sigma
    result = jnp.where(occupied, stacked[:, :channels].astype(F32) + silu, 0.0).astype(BF)
    res_o[0] = result.reshape(planes, edge, edge, channels)
    column = pl.ds(pl.multiple_of(x0 * edge, cols), cols)
    spread = colg_o[column].reshape(cols, 1, channels)
    grad_result = gout[s, pl.ds(x0, planes)].astype(F32).reshape(cols, edge, channels) + spread
    slope = sigma * (1.0 + (preact - silu))
    gpre = jnp.where(occupied, grad_result.reshape(rows, channels) * slope, 0.0).astype(BF)
    gtile = gpre.reshape(planes, edge, edge, channels)
    gpre_o[0] = gtile
    for upper, step, layer in ((0, 0, 0), (1, steps - 1, planes - 1)):
        for phase, out in ((0, gx0_o), (1, gx1_o)):
            @pl.when((xi == step) & ((lax.axis_index("mx") % 2 == phase) == bool(upper)))
            def _(out=out, layer=layer):
                out[s] = gtile[layer]

    even = lax.axis_index("my") % 2 == 0
    low, high = gtile[:, 0], gtile[:, edge - 1]
    gy0_o[s, pl.ds(x0, planes)] = jnp.where(even, high, low)
    gy1_o[s, pl.ds(x0, planes)] = jnp.where(even, low, high)

    of_row = lax.broadcasted_iota(jnp.int32, (cols, rows), 1) // edge
    pool = (of_row == lax.broadcasted_iota(jnp.int32, (cols, rows), 0)).astype(BF)
    colsum[column] += jnp.dot(pool, result, preferred_element_type=F32)
    tail = (taps + 1) * channels
    pay_o[tail : tail + 1] += jnp.sum(gpre.astype(F32), axis=0, keepdims=True)
    turned[...] = gpre.T
    zlow[...] = stacked[:, 5 * channels : 6 * channels]
    zhigh[...] = stacked[:, 6 * channels : 7 * channels]

    @pl.when((s == slots - 1) & (xi == steps - 1))
    def _():
        add_weight_terms(acc, turned, vol, zlow, zhigh, s, x0, planes)
        for t in range(taps):
            at = slice(t * channels, (t + 1) * channels)
            pay_o[at] = acc[:, at].T
        column_bf = (colsum[...] * scale).astype(BF)
        head_o[...] = jnp.dot(column_bf, hw[...], preferred_element_type=F32).astype(BF)
        pay_o[taps * channels : tail] = lax.dot_general(
            column_bf, ghead[...], (((0,), (0,)), ((), ())), preferred_element_type=F32
        )


def backward_kernel(first, total, meta, grad, x0f, x1f, y0f, y1f, wt_in, gout_in, colg_in, *rest):
    out_o, vol, zbuf, wt, colg, gout, sems, loads = rest[-8:]
    slots, edge, channels = grad.shape[0], grad.shape[1], grad.shape[4]
    planes, held = out_o.shape[1], vol.shape[1] - 2
    steps = held // planes
    s, xi = pl.program_id(0), pl.program_id(1)

    small = [
        pltpu.make_async_copy(wt_in, wt, loads.at[0]),
        pltpu.make_async_copy(colg_in, colg, loads.at[1]),
    ]

    def upstream(of_slot, step):
        local = pl.ds(step * planes, planes)
        return pltpu.make_async_copy(
            gout_in.at[of_slot, pl.ds(first + step * planes, planes)],
            gout.at[of_slot, local],
            loads.at[2 + of_slot * steps + step],
        )

    below, above = min(first, 1), min(edge - first - held, 1)
    cut = min(planes + 1, held)
    parts = [
        [
            pltpu.make_async_copy(
                grad.at[i, first + lo : first + hi],
                vol.at[i, 1 + lo : 1 + hi, 1 : edge + 1],
                sems.at[slots * (4 + h) + i],
            )
            for i in range(slots)
        ]
        for h, (lo, hi) in enumerate(((-below, cut), (cut, held + above)))
    ]

    @pl.when((s == 0) & (xi == 0))
    def _():
        found = halo_copies(meta, slots, (x0f, x1f, y0f, y1f), vol, sems, first, held, edge, True)
        for copy in parts[0]:
            copy.start()
        start_halos(found, vol)
        for copy in small:
            copy.start()
        upstream(0, 0).start()
        for copy in parts[1]:
            copy.start()
        for of_slot in range(slots):
            for step in range(steps):
                if (of_slot, step) != (0, 0):
                    upstream(of_slot, step).start()
        for copy in parts[0] + small:
            copy.wait()
        wait_halos(found)

    @pl.when((s == 0) & (xi == 1))
    def _():
        for copy in parts[1]:
            copy.wait()

    upstream(s, xi).wait()
    rows = planes * edge * edge
    cols = planes * edge
    stacked = windows(meta, vol, zbuf, s, xi * planes, planes, -1)
    conv = jnp.dot(stacked, wt[...], preferred_element_type=F32)
    column = pl.ds(pl.multiple_of(first * edge + xi * cols, cols), cols)
    spread = colg[column].reshape(cols, 1, channels)
    grad_result = gout[s, pl.ds(xi * planes, planes)].astype(F32).reshape(cols, edge, channels) + spread
    total = jnp.where(s < total[0], grad_result.reshape(rows, channels) + conv, 0.0).astype(BF)
    out_o[0] = total.reshape(planes, edge, edge, channels)


def in_hbm(x):
    return pltpu.with_memory_space_constraint(x, pltpu.HBM)


def swap(x, axis, odd):
    pairs = []
    for i in range(odd, lax.axis_size(axis) - 1, 2):
        pairs += [(i, i + 1), (i + 1, i)]
    return lax.ppermute(x, axis, pairs)


def swap_faces(sent, axis):
    arrived = []
    for odd in range(2):
        arrived.append(swap(sent[odd], axis, odd))
    return arrived


def turn(x, axis, by):
    count = lax.axis_size(axis)
    return lax.ppermute(x, axis, [(i, (i + by) % count) for i in range(count)])


def turn_faces(sent, axis):
    arrived = []
    for i, by in enumerate((1, -1)):
        arrived.append(turn(sent[i], axis, by))
    return arrived


def partner(x, axis, bit):
    return lax.ppermute(x, axis, [(i, i ^ (1 << bit)) for i in range(lax.axis_size(axis))])


def own_bit(axis, bit):
    return (lax.axis_index(axis) >> bit) & 1


def halved(x, axis, bit):
    me = own_bit(axis, bit)
    parts = x.reshape((2, x.shape[0] // 2) + x.shape[1:])
    own = lax.dynamic_index_in_dim(parts, me, 0, False)
    sent = lax.dynamic_index_in_dim(parts, 1 - me, 0, False)
    return own + partner(sent.astype(BF), axis, bit).astype(F32)


def summed(x, axis, bit):
    return x + partner(x.astype(BF), axis, bit).astype(F32)


def bits(axis):
    return range((lax.axis_size(axis) - 1).bit_length())


def all_summed(x):
    x = halved(x, "region", 0)
    later = [(axis, b) for axis in ("mx", "my") for b in bits(axis) if b]
    for axis, bit in [("mx", 0), ("my", 0)] + sorted(later, key=lambda stage: stage[1]):
        x = summed(x, axis, bit)
    x = x.astype(BF)
    return x, partner(x, "region", 0)


def body(
    features_in, conv_weight, conv_bias, head_weight, grad_out, grad_head, block_count, neighbours
):
    blocks = features_in.reshape(features_in.shape[3:])
    upstream = grad_out.reshape(grad_out.shape[3:])
    head_grad = grad_head.reshape(grad_head.shape[3:])
    slots, edge, channels = blocks.shape[0], blocks.shape[1], blocks.shape[4]
    taps = conv_weight.shape[0]
    meta = (block_count.reshape(1), neighbours.reshape(-1))
    anywhere = pl.BlockSpec(memory_space=pl.ANY)
    hbm = pl.BlockSpec(memory_space=pltpu.HBM)
    vmem = pl.BlockSpec(memory_space=pltpu.VMEM)
    face = jax.ShapeDtypeStruct((slots, edge, edge, channels), BF)
    sent = pl.pallas_call(
        pick_kernel,
        in_specs=[hbm],
        out_specs=[vmem] * 4,
        scratch_shapes=[pltpu.SemaphoreType.DMA((4,))],
        out_shape=[face] * 4,
        compiler_params=pltpu.CompilerParams(vmem_limit_bytes=8 << 20),
        name="pick",
    )(in_hbm(blocks))
    faces = turn_faces(sent[:2], "mx") + turn_faces(sent[2:], "my")

    whole = lambda *shape: pl.BlockSpec(shape, lambda i, j, m, n: (0,) * len(shape))
    tile = pl.BlockSpec((1, PLANES, edge, edge, channels), lambda i, j, m, n: (i, j, 0, 0, 0))
    volume = (slots, edge, edge, edge, channels)
    padded = pltpu.VMEM((slots, edge + 2, edge + 2, edge, channels), BF)
    columns = edge * edge
    pay_rows = ((taps + 1) * channels // 32 + 1) * 32
    flops = 2 * slots * edge**3 * taps * channels * channels
    moved = slots * edge**3 * channels * 2
    params = pltpu.CompilerParams(
        dimension_semantics=("arbitrary", "arbitrary"), vmem_limit_bytes=GRANT
    )
    result, head_tile, gpre, gx0, gx1, gy0, gy1, colg, pay = pl.pallas_call(
        forward_kernel,
        grid_spec=pltpu.PrefetchScalarGridSpec(
            num_scalar_prefetch=2,
            grid=(slots, edge // PLANES),
            in_specs=[
                hbm, anywhere, anywhere, anywhere, anywhere,
                *[anywhere] * 5,
            ],
            out_specs=[
                tile, whole(columns, channels), tile,
                *[whole(slots, edge, edge, channels)] * 4,
                whole(columns, channels), whole(pay_rows, channels),
            ],
            scratch_shapes=[
                padded, pltpu.VMEM((PLANES * edge, edge + 16, channels), F32),
                pltpu.VMEM((columns, channels), F32),
                pltpu.VMEM((channels, taps * channels), F32),
                pltpu.VMEM((channels, PLANES * columns), BF),
                pltpu.VMEM((PLANES * columns, channels), BF),
                pltpu.VMEM((PLANES * columns, channels), BF),
                pltpu.VMEM((taps * channels, channels), BF),
                pltpu.VMEM((1, channels), F32),
                pltpu.VMEM((channels, channels), BF),
                pltpu.VMEM((columns, channels), BF),
                pltpu.VMEM(volume, BF),
                pltpu.SemaphoreType.DMA((slots * 6,)),
                pltpu.SemaphoreType.DMA((4 + slots * (edge // PLANES),)),
            ],
        ),
        out_shape=[
            pltpu.HBM(volume, BF),
            jax.ShapeDtypeStruct((columns, channels), BF),
            pltpu.HBM(volume, BF),
            *[face] * 4,
            jax.ShapeDtypeStruct((columns, channels), F32),
            jax.ShapeDtypeStruct((pay_rows, channels), F32),
        ],
        compiler_params=params,
        cost_estimate=pl.CostEstimate(
            flops=2 * flops, bytes_accessed=5 * moved, transcendentals=moved // 2
        ),
        name="forward",
    )(
        *meta, in_hbm(blocks), *faces, in_hbm(conv_weight.reshape(taps * channels, channels)),
        conv_bias.reshape(1, channels), in_hbm(head_weight), in_hbm(upstream), in_hbm(head_grad),
    )

    grad_faces = swap_faces((gx0, gx1), "mx") + swap_faces((gy0, gy1), "my")
    turned = jnp.transpose(conv_weight, (0, 2, 1)).reshape(taps * channels, channels)
    grad_local = None
    pieces = edge // PIECE
    for k in range(pieces):
        part = pl.BlockSpec(
            (1, STEP, edge, edge, channels),
            lambda i, j, m, n, k=k: (i, k * (PIECE // STEP) + j, 0, 0, 0),
        )
        operands = [*meta, in_hbm(gpre), *grad_faces, turned, in_hbm(upstream), colg]
        specs = [hbm] + [anywhere] * 4
        specs += [anywhere, hbm, anywhere]
        if grad_local is not None:
            operands.append(grad_local)
            specs.append(hbm)
        grad_local = pl.pallas_call(
            functools.partial(backward_kernel, k * PIECE),
            grid_spec=pltpu.PrefetchScalarGridSpec(
                num_scalar_prefetch=2,
                grid=(slots, PIECE // STEP),
                in_specs=specs,
                out_specs=part,
                scratch_shapes=[
                    pltpu.VMEM((slots, PIECE + 2, edge + 2, edge, channels), BF),
                    pltpu.VMEM((STEP * edge, edge + 16, channels), F32),
                    pltpu.VMEM((taps * channels, channels), BF),
                    pltpu.VMEM((columns, channels), F32),
                    pltpu.VMEM((slots, PIECE, edge, edge, channels), BF),
                    pltpu.SemaphoreType.DMA((slots * 6,)),
                    pltpu.SemaphoreType.DMA((2 + slots * (PIECE // STEP),)),
                ],
            ),
            out_shape=jax.ShapeDtypeStruct(volume, BF),
            input_output_aliases={len(operands) - 1: 0} if k else {},
            compiler_params=pltpu.CompilerParams(
                dimension_semantics=("arbitrary", "arbitrary"), vmem_limit_bytes=GRANT
            ),
            cost_estimate=pl.CostEstimate(
                flops=flops // pieces, bytes_accessed=4 * moved // pieces, transcendentals=0
            ),
        )(*operands)

    own, other = all_summed(pay)
    conv_rows = taps * channels
    grad_conv, grad_bias, grad_head_weight = pl.pallas_call(
        finish_kernel,
        in_specs=[vmem] * 2,
        out_specs=[vmem] * 3,
        out_shape=[
            jax.ShapeDtypeStruct((conv_rows, channels), F32),
            jax.ShapeDtypeStruct((1, channels), F32),
            jax.ShapeDtypeStruct((channels, channels), F32),
        ],
        compiler_params=pltpu.CompilerParams(vmem_limit_bytes=8 << 20),
        name="finish",
    )(own, other)
    return (
        result.reshape(features_in.shape),
        head_tile.reshape(grad_head.shape),
        grad_local.reshape(features_in.shape),
        grad_conv.reshape(conv_weight.shape),
        grad_bias.reshape(channels),
        grad_head_weight,
    )


def solution(mesh):
    tiles = P("region", "mx", "my", None, None, None, None, None)
    rows = P("region", "mx", "my", None, None)

    return jax.shard_map(
        body,
        mesh=mesh,
        in_specs=(tiles, P(), P(), P(), tiles, rows, P("region", "mx", "my"), rows),
        out_specs=(tiles, rows, tiles, P(), P(), P()),
        check_vma=False,
    )
```
